256 devices in a mesh: ctx: 64 (over z, x, core), head: 4 (over y).
Axes of the slice: x: 4, y: 4, z: 8, core: 2. Of those that a mesh axis runs over, the one named last changes fastest.
Arguments:
- inputs: bfloat16 [12288, 2048], P('ctx'), may hold values from -6 to 6
- projection: bfloat16 [3, 2048, 1024], P(None, None, 'head'), may hold values from -0.125 to 0.125
- conv_weight: float32 [3, 4, 1024], P(None, None, 'head'), may hold values from -3 to 3
- gate_code: int32 [8, 12288], P('head', 'ctx'), may hold values from 0 to 1023
- beta_code: int32 [8, 12288], P('head', 'ctx'), may hold values from 0 to 1023
- grad_out: bfloat16 [12288, 1024], P('ctx', 'head'), may hold values from -6 to 6
Outputs:
- input_grad: bfloat16 [12288, 2048], P(('ctx', 'head'))
- kernel_grad: float32 [3, 4, 1024], P(None, None, 'head')
The draws below stay inside these ranges and needn't reach their ends.
All inputs are finite; a program needn't handle non-finite values.
Results may differ from the reference program's by a relative error of at most 0.0068.
The reference program's roundings to bfloat16 on the way (of `projected` and `rounded`) count: a program that leaves them out, or rounds other values in their place, can miss the bound.
Values may be sent and summed in bfloat16 or wider, within the bound.
No kernel may reach another device: no remote copies, remote signals or barrier semaphores. Data moves between devices by JAX's collectives and lax.ppermute only.
A program may use at most 64 MiB of HBM per device.

```python
import jax
import jax.numpy as jnp
from jax import lax

D = 2048
H = 8
DK = 128
KW = 4
GROUP = 64
HD = 1024
TOKENS = 12288


def draw_codes(key, offset_salt, slow_level):
    ranking_key, value_key = jax.random.split(jax.random.fold_in(key, offset_salt))
    ranking = jax.random.permutation(ranking_key, H)
    levels = jnp.where(ranking < H // 2, slow_level, 1024).astype(jnp.int32)
    code_values = jax.random.randint(value_key, (H, TOKENS), 0, 1024, dtype=jnp.int32) % levels[:, None]
    code_values = code_values.at[:, 0].set(0)
    code_values = code_values.at[:, 1].set(levels - 1)
    return code_values.astype(jnp.int32)


def draw_gate_code(key, part):
    return draw_codes(key, 101, 3)


def draw_beta_code(key, part):
    return draw_codes(key, 202, 17)


def level_of(own_key, dims, cuts, least, high):
    gain = 1.0
    for axis_at, blocks in cuts:
        heights = jax.random.uniform(jax.random.fold_in(jax.random.fold_in(own_key, 6), axis_at), (blocks,), jnp.float32, least / len(cuts), high / len(cuts))
        gain = gain * jnp.repeat(jnp.exp(heights), dims[axis_at] // blocks).reshape((-1,) + (1,) * (len(dims) - 1 - axis_at))
    return gain


def bell_draw(stream_key, shape, scale, bound, cuts=(), held_as=jnp.bfloat16):
    values = jax.random.normal(stream_key, shape, jnp.float32) * scale
    if len(cuts) > 0:
        values = level_of(stream_key, shape, cuts, -0.22, 0.18) * values
    return jnp.clip(values, min=-bound, max=bound).astype(held_as)


def setup_inputs(seed: int = 0) -> dict:
    seeds = jax.random.split(jax.random.key(seed), 7)
    inputs = bell_draw(seeds[0], (TOKENS, D), 1.0, 6.0, ((0, 64),))
    projection = bell_draw(seeds[1], (3, D, HD), D ** -0.5, 0.125, ((2, 4),))
    conv_weight = bell_draw(seeds[2], (3, KW, HD), KW ** -0.5, 3.0, ((2, 4),), jnp.float32)
    gate_code = draw_gate_code(jax.random.fold_in(seeds[6], 71), 0)
    beta_code = draw_beta_code(jax.random.fold_in(seeds[6], 71), 0)
    grad_out = bell_draw(seeds[5], (TOKENS, HD), 1.0, 6.0, ((0, 64), (1, 4)))
    return {"inputs": inputs, "projection": projection, "conv_weight": conv_weight, "gate_code": gate_code, "beta_code": beta_code, "grad_out": grad_out}


HIGHEST_PRECISION = lax.Precision.HIGHEST

def normalize(matrix):
    return matrix * lax.rsqrt(lax.optimization_barrier(jnp.sum(matrix * matrix, -1, keepdims=True)) + 1e-06)

def features(extended, weights):
    length = extended.shape[1] - (KW - 1)
    convolved = weights[:, 0:1, :] * extended[:, 0:length, :]
    for offset in range(1, KW):
        convolved = convolved + weights[:, offset:offset + 1, :] * extended[:, offset:offset + length, :]
    activated = jax.nn.silu(convolved)
    head_count = activated.shape[2] // DK
    activated = activated.reshape(3, length, head_count, DK).transpose(0, 2, 1, 3)
    queries = normalize(activated[0]) * DK ** (-0.5)
    norm_keys = normalize(activated[1])
    return (queries, norm_keys, activated[2])

def block_step(carried, pieces):
    queries, norm_keys, value_rows, log_gate, beta_rate = pieces
    cumulative = jnp.cumsum(log_gate, axis=-1)
    decay_now = jnp.exp(cumulative)
    between = cumulative[:, :, None] - cumulative[:, None, :]
    position = jnp.arange(log_gate.shape[-1])
    strict = position[:, None] > position[None, :]
    inclusive = position[:, None] >= position[None, :]
    key_gram = jnp.einsum('htd,hsd->hts', norm_keys, norm_keys, precision=HIGHEST_PRECISION)
    lower_part = jnp.where(strict, jnp.exp(between), 0.0) * key_gram * beta_rate[:, :, None]
    recalled = jnp.einsum('htd,hvd->htv', norm_keys, carried, precision=HIGHEST_PRECISION)
    target = beta_rate[:, :, None] * (value_rows - decay_now[:, :, None] * recalled)
    pseudo = jax.scipy.linalg.solve_triangular(lower_part, target, lower=True, unit_diagonal=True)
    scores = jnp.einsum('htd,hsd->hts', queries, norm_keys, precision=HIGHEST_PRECISION) * jnp.where(inclusive, jnp.exp(between), 0.0)
    outputs = decay_now[:, :, None] * jnp.einsum('htd,hvd->htv', queries, carried, precision=HIGHEST_PRECISION)
    outputs = outputs + jnp.einsum('hts,hsv->htv', scores, pseudo, precision=HIGHEST_PRECISION)
    group_total = cumulative[:, -1]
    remaining = jnp.exp(group_total[:, None] - cumulative)
    new_state = jnp.exp(group_total)[:, None, None] * carried
    new_state = new_state + jnp.einsum('hsv,hsd->hvd', pseudo, remaining[:, :, None] * norm_keys, precision=HIGHEST_PRECISION)
    return (new_state, outputs)

def run_blocks(queries, norm_keys, value_rows, log_gate, beta_rate, carried):
    head_count = queries.shape[0]
    length = queries.shape[1]
    blocks = length // GROUP

    def to_blocks(tensor):
        return jnp.moveaxis(tensor.reshape((tensor.shape[0], blocks, GROUP) + tensor.shape[2:]), 1, 0)
    final_state, outputs = lax.scan(jax.checkpoint(block_step), carried, (to_blocks(queries), to_blocks(norm_keys), to_blocks(value_rows), to_blocks(log_gate), to_blocks(beta_rate)))
    outputs = jnp.moveaxis(outputs, 0, 1).reshape(head_count, length, DK)
    return (outputs, final_state)

def reference(inputs, projection, conv_weight, gate_code, beta_code, grad_out):
    projected = jnp.stack([jnp.dot(inputs.astype(jnp.float32), projection[member].astype(jnp.float32), preferred_element_type=jnp.float32) for member in range(3)]).astype(jnp.bfloat16)
    log_gate = jnp.log(1.0 - 0.001 * gate_code.astype(jnp.float32) / 1023.0)
    beta_rate = beta_code.astype(jnp.float32) / 1023.0

    def forward(raw_float, weights):
        extended = jnp.pad(raw_float, ((0, 0), (KW - 1, 0), (0, 0)))
        queries, norm_keys, value_rows = features(extended, weights)
        outputs, final_state = run_blocks(queries, norm_keys, value_rows, log_gate, beta_rate, jnp.zeros((H, DK, DK), jnp.float32))
        return outputs
    primal, pullback = jax.vjp(forward, projected.astype(jnp.float32), conv_weight)
    cotangent = grad_out.astype(jnp.float32).reshape(TOKENS, H, DK).transpose(1, 0, 2)
    raw_grad, weight_grad = pullback(cotangent)
    rounded = raw_grad.astype(jnp.bfloat16)
    input_grad = jnp.einsum('mtc,mdc->td', rounded.astype(jnp.float32), projection.astype(jnp.float32), preferred_element_type=jnp.float32)
    return (input_grad.astype(jnp.bfloat16), weight_grad)
```

```python
import functools

import jax
import jax.numpy as jnp
from jax import lax
from jax.experimental import pallas as pl
from jax.experimental.pallas import tpu as pltpu
from jax.sharding import PartitionSpec as P

DK = 128
KW = 4
BLOCK = 64
XS = 4
SCALE = DK**-0.5
F32 = jnp.float32
BF16 = jnp.bfloat16
HIGHEST = lax.Precision.HIGHEST
NN = (((1,), (0,)), ((), ()))
NT = (((1,), (1,)), ((), ()))
TN = (((0,), (0,)), ((), ()))


def split(a):
    high = a.astype(BF16)
    return high, (a - high.astype(F32)).astype(BF16)


def dot(a, b, dims):
    return lax.dot_general(a, b, dims, preferred_element_type=F32)


def mm(a, b, dims=NN):
    ah, al = split(a)
    bh, bl = split(b)
    return dot(ah, bh, dims) + (dot(ah, bl, dims) + dot(al, bh, dims))


def mm_left(a, b, dims=NN):
    ah, al = split(a)
    return dot(ah, b, dims) + dot(al, b, dims)


def mm_right(a, b, dims=NN):
    bh, bl = split(b)
    return dot(a, bh, dims) + dot(a, bl, dims)


def exact(a, b, dims):
    return lax.dot_general(a, b, dims, precision=HIGHEST, preferred_element_type=F32)


def iotas(rows, cols):
    return (
        lax.broadcasted_iota(jnp.int32, (rows, cols), 0),
        lax.broadcasted_iota(jnp.int32, (rows, cols), 1),
    )


def eye(n):
    r, c = iotas(n, n)
    return (r == c).astype(F32)


def call(kernel, out_shape, scratch=(), smem=0, flops=0, **kw):
    def run(*args):
        specs = [
            pl.BlockSpec(memory_space=pltpu.SMEM if i < smem else pltpu.VMEM)
            for i in range(len(args))
        ]
        return pl.pallas_call(
            kernel,
            out_shape=out_shape,
            in_specs=specs,
            out_specs=jax.tree.map(lambda _: pl.BlockSpec(memory_space=pltpu.VMEM), out_shape),
            scratch_shapes=list(scratch),
            cost_estimate=pl.CostEstimate(
                flops=flops, bytes_accessed=4_000_000, transcendentals=0
            ),
            **kw,
        )(*args)

    return run


def shape(s, d=F32):
    return jax.ShapeDtypeStruct(s, d)


def project_kernel(x_ref, w_ref, o_ref, tail_ref):
    value = dot(x_ref[...], w_ref[0], NN).astype(BF16)
    o_ref[0] = value
    rows = value.shape[0]
    tail_ref[0] = value[rows - 16 :].astype(F32)[8:]


def sigmoid(z):
    return 1.0 / (1.0 + jnp.exp(-z))


def local_kernel(
    me_ref, proj_ref, halo_ref, cw_ref, gate_ref, beta_ref, grad_ref,
    keep_ref, send_ref, z_ref, q_ref, k_ref, w_ref, u_ref, p_ref, d_ref, a_ref, t_ref, col_ref,
    ext, buf,
):
    rows = proj_ref.shape[1]
    blocks = rows // BLOCK
    for m in range(3):
        ext[m, 0:8] = halo_ref[m]
        ext[m, 8 : 8 + rows] = proj_ref[m].astype(F32)
    act = []
    for m in range(3):
        z = cw_ref[m, 0:1] * ext[m, 5 : 5 + rows]
        for j in range(1, KW):
            z = z + cw_ref[m, j : j + 1] * ext[m, 5 + j : 5 + j + rows]
        z_ref[m] = z
        act.append(z * sigmoid(z))
    logs = jnp.log(1.0 - 0.001 * gate_ref[...].astype(F32) / 1023.0)
    beta = beta_ref[...].astype(F32) / 1023.0
    r, c = iotas(rows, rows)
    tri = (r >= c).astype(F32)
    col = exact(tri, logs, NT)
    row = exact(logs, tri, NT)
    betas = exact((r == c).astype(F32), beta, NT)
    r64, c64 = iotas(BLOCK, BLOCK)
    diag = []
    keys = []
    queries = []
    for h in range(2):
        lanes = slice(h * DK, (h + 1) * DK)
        aq = act[0][:, lanes]
        ak = act[1][:, lanes]
        queries.append(aq * lax.rsqrt(jnp.sum(aq * aq, -1, keepdims=True) + 1e-06) * SCALE)
        keys.append(ak * lax.rsqrt(jnp.sum(ak * ak, -1, keepdims=True) + 1e-06))
        b = col[:, h : h + 1]
        bt = betas[:, h : h + 1]
        decay = jnp.where(r >= c, jnp.exp(b - row[h : h + 1]), 0.0)
        d_ref[h] = decay
        gram = mm(keys[h], keys[h], NT)
        a_ref[h] = jnp.where(r > c, decay * gram * bt, 0.0)
        p_ref[h] = decay * mm(queries[h], keys[h], NT)
        q_ref[h] = queries[h]
        k_ref[h] = keys[h]
        total = col[rows - 1 : rows, h : h + 1]
        col_ref[h, 0] = jnp.broadcast_to(jnp.exp(b), (rows, DK))
        col_ref[h, 1] = jnp.broadcast_to(bt, (rows, DK))
        col_ref[h, 2] = jnp.broadcast_to(jnp.exp(total - b), (rows, DK))
        for i in range(blocks):
            span = slice(i * BLOCK, (i + 1) * BLOCK)
            kb = keys[h][span]
            rb = exact(logs, tri[span], NT)[h : h + 1]
            dec = jnp.exp(b[span] - rb)
            diag.append(jnp.where(r64 > c64, dec * mm(kb, kb, NT) * bt[span], 0.0))
    lower = jnp.stack(diag)
    count = len(diag)
    tiles = []
    for k in range(BLOCK // 8):
        rr = lax.broadcasted_iota(jnp.int32, (count, 8, BLOCK), 1) + 8 * k
        cc = lax.broadcasted_iota(jnp.int32, (count, 8, BLOCK), 2)
        tiles.append((rr == cc).astype(F32))
    for s in range(BLOCK - 1):
        k0, r0 = divmod(s, 8)
        pivot = tiles[k0][:, r0 : r0 + 1, :]
        for k in range(k0, BLOCK // 8):
            tiles[k] = tiles[k] - lower[:, 8 * k : 8 * k + 8, s : s + 1] * pivot
    inverse = jnp.concatenate(tiles, 1)
    for h in range(2):
        for i in range(blocks):
            t_ref[h, i] = inverse[h * blocks + i]
    for h in range(2):
        lanes = slice(h * DK, (h + 1) * DK)
        eb = col_ref[h, 0]
        bt = col_ref[h, 1]
        rest = col_ref[h, 2]
        rhs = jnp.concatenate([bt * eb * keys[h], bt * act[2][:, lanes]], 1)
        done = []
        for i in range(blocks):
            span = slice(i * BLOCK, (i + 1) * BLOCK)
            part = rhs[span]
            if i > 0:
                past = jnp.concatenate(done, 0) if i > 1 else done[0]
                part = part - mm(a_ref[h, span, 0 : i * BLOCK], past)
            done.append(mm(inverse[h * blocks + i], part))
        wu = jnp.concatenate(done, 0)
        w = wu[:, :DK]
        w_ref[h] = w
        u_ref[h] = wu[:, DK:]
        kt = rest * keys[h]
        ml = mm(wu, kt, TN)
        buf[h, 0] = eb[rows - 1 : rows] * eye(DK) - ml[:DK]
        buf[h, 1] = ml[DK:]
        effective = eb * queries[h] - mm(p_ref[h], w)
        buf[h, 2] = mm_right(grad_ref[:, lanes], effective, TN)
    core = me_ref[0]
    keep_ref[...] = buf[core]
    send_ref[...] = buf[1 - core]


def adjoint_kernel(p_ref, a_ref, t_ref, k_ref, col_ref, grad_ref, dr_ref, e_ref):
    rows = k_ref.shape[1]
    blocks = rows // BLOCK
    for h in range(2):
        lanes = slice(h * DK, (h + 1) * DK)
        back = mm_left(p_ref[h], grad_ref[:, lanes], TN)
        rhs = jnp.concatenate([back, col_ref[h, 2] * k_ref[h]], 1)
        done = {}
        for i in reversed(range(blocks)):
            span = slice(i * BLOCK, (i + 1) * BLOCK)
            part = rhs[span]
            for j in range(i + 1, blocks):
                below = slice(j * BLOCK, (j + 1) * BLOCK)
                wide = mm(a_ref[h, below], done[j], TN)
                part = part - wide[span]
            done[i] = mm(t_ref[h, i], part, TN)
        full = jnp.concatenate([done[i] for i in range(blocks)], 0)
        dr_ref[h] = full[:, :DK]
        e_ref[h] = full[:, DK:]


def ordered_pair(me_ref, keep_ref, recv_ref):
    first = me_ref[0] == 0
    keep, recv = keep_ref[...], recv_ref[...]
    return jnp.where(first, keep, recv), jnp.where(first, recv, keep)


def pair_kernel(me_ref, keep_ref, recv_ref, out_ref):
    e0, e1 = ordered_pair(me_ref, keep_ref, recv_ref)
    both = mm(jnp.concatenate([e0[0], e0[1]], 0), e1[0])
    m = (both[:DK] - eye(DK)).astype(BF16)
    s = (both[DK:] + e1[1]).astype(BF16)
    g = (mm(e1[2], e0[0], NT) + e0[2]).astype(BF16)
    for k in range(XS):
        out_ref[k, 0] = m
        out_ref[k, 1] = s
        out_ref[k, 2] = g


def group_kernel(me_ref, in_ref, pre_ref, suf_ref, out_ref):
    x = me_ref[1]
    z = me_ref[2]
    one = eye(DK)
    zero = jnp.zeros((DK, DK), F32)

    def put(ref, value):
        ref[0] = value[:DK]
        ref[1] = value[DK:]

    start = jnp.concatenate([one, zero], 0)
    fwd = start
    bwd = start
    for step in range(XS):
        j = step

        @pl.when(x == j)
        def _(fwd=fwd):
            put(pre_ref, fwd)

        @pl.when(x == XS - 1 - j)
        def _(bwd=bwd):
            put(suf_ref, bwd)

        mf = in_ref[j, 0]
        mb = in_ref[XS - 1 - j, 0]
        lf = in_ref[j, 1].astype(F32)
        gb = in_ref[XS - 1 - j, 2].astype(F32)
        if step == 0:
            fwd = jnp.concatenate([one + mf.astype(F32), lf], 0)
            bwd = jnp.concatenate([one + mb.astype(F32).T, gb], 0)
        else:
            fwd = fwd + mm_left(fwd, mf, NN) + jnp.concatenate([zero, lf], 0)
            bwd = bwd + mm_left(bwd, mb, NT) + jnp.concatenate([zero, gb], 0)
    m = (fwd[:DK] - one).astype(BF16)
    s = fwd[DK:]
    g = bwd[DK:]
    for p in range(out_ref.shape[0]):
        out_ref[p, 0] = m
        out_ref[p, 1] = jnp.where(p > z, s, g).astype(BF16)


def enter_kernel(me_ref, in_ref, pre_ref, suf_ref, keep_ref, recv_ref, own_ref, send_ref):
    z = me_ref[2]
    groups = in_ref.shape[0]
    s = jnp.zeros((DK, DK), F32)
    g = jnp.zeros((DK, DK), F32)
    for step in range(groups - 1):
        q = step
        t = groups - 1 - step
        lq = in_ref[q, 1].astype(F32)
        gt = in_ref[t, 1].astype(F32)
        if step == 0:
            s = jnp.where(q < z, lq, s)
            g = jnp.where(t > z, gt, g)
        else:
            s = jnp.where(q < z, s + mm_left(s, in_ref[q, 0], NN) + lq, s)
            g = jnp.where(t > z, g + mm_left(g, in_ref[t, 0], NT) + gt, g)
    s = mm(s, pre_ref[0]) + pre_ref[1]
    g = mm(g, suf_ref[0]) + suf_ref[1]
    e0, e1 = ordered_pair(me_ref, keep_ref, recv_ref)
    s1 = mm(s, e0[0]) + e0[1]
    g0 = mm(g, e1[0], NT) + e1[2]
    first = me_ref[0] == 0
    own_ref[0] = jnp.where(first, s, s1)
    own_ref[1] = jnp.where(first, g0, g)
    send_ref[0] = jnp.where(first, s1, s)
    send_ref[1] = jnp.where(first, g, g0)


def backward_kernel(
    me_ref, own_ref, recv_ref, proj_ref, halo_ref, cw_ref, grad_ref,
    z_ref, q_ref, k_ref, w_ref, u_ref, d_ref, col_ref, dr_ref, e_ref,
    out_ref, tail_ref, spill_ref, taps_ref,
    ext, dzs,
):
    rows = proj_ref.shape[1]
    core = me_ref[0]
    r, c = iotas(rows, rows)
    pads = jnp.zeros((8, dzs.shape[2]), F32)
    for m in range(3):
        ext[m, 0:8] = halo_ref[m]
        ext[m, 8 : 8 + rows] = proj_ref[m].astype(F32)
        dzs[m, 0:8] = pads
        dzs[m, 8 + rows : 16 + rows] = pads
    for h in range(2):
        lanes = slice(h * DK, (h + 1) * DK)
        mine = core == h
        s = jnp.where(mine, own_ref[0], recv_ref[0])
        g = jnp.where(mine, own_ref[1], recv_ref[1])
        q, k = q_ref[h], k_ref[h]
        eb, bt, rest = col_ref[h, 0], col_ref[h, 1], col_ref[h, 2]
        do = grad_ref[:, lanes].astype(F32)
        u = u_ref[h] - mm(w_ref[h], s, NT)
        dr = dr_ref[h] + mm(e_ref[h], g, NT)
        cross = mm(jnp.concatenate([do, dr], 0), u, NT)
        decay = d_ref[h]
        x1 = decay * cross[:rows]
        da = jnp.where(r > c, decay * cross[rows:], 0.0) * -bt[:, :1]
        outer = mm(jnp.concatenate([eb * do, -(bt * eb) * dr], 0), s)
        right = mm(jnp.concatenate([x1, da], 0), k)
        dq = outer[:rows] + right[:rows]
        dk = outer[rows:] + right[rows:] + rest * mm(u, g)
        dk = dk + mm(jnp.concatenate([x1, da], 0), jnp.concatenate([q, k], 0), TN)
        dv = bt * dr
        zq = z_ref[0, :, lanes]
        zk = z_ref[1, :, lanes]
        zv = z_ref[2, :, lanes]
        sq, sk, sv = sigmoid(zq), sigmoid(zk), sigmoid(zv)
        aq, ak = zq * sq, zk * sk
        rq = lax.rsqrt(jnp.sum(aq * aq, -1, keepdims=True) + 1e-06)
        rk = lax.rsqrt(jnp.sum(ak * ak, -1, keepdims=True) + 1e-06)
        daq = rq * (SCALE * dq - q * (jnp.sum(q * dq, -1, keepdims=True) * (1.0 / SCALE)))
        dak = rk * (dk - k * jnp.sum(k * dk, -1, keepdims=True))
        dzs[0, 8 : 8 + rows, lanes] = daq * (sq * (1.0 + zq * (1.0 - sq)))
        dzs[1, 8 : 8 + rows, lanes] = dak * (sk * (1.0 + zk * (1.0 - sk)))
        dzs[2, 8 : 8 + rows, lanes] = dv * (sv * (1.0 + zv * (1.0 - sv)))
    for m in range(3):
        dz = dzs[m, 8 : 8 + rows]
        dx = None
        spill = None
        for j in range(KW):
            tap = cw_ref[m, j : j + 1]
            term = tap * dzs[m, 11 - j : 11 - j + rows]
            first = tap * dzs[m, 3 - j : 11 - j]
            dx = term if dx is None else dx + term
            spill = first if spill is None else spill + first
            taps_ref[m, j : j + 1] = jnp.sum(dz * ext[m, 5 + j : 5 + j + rows], 0, keepdims=True)
        out_ref[m] = dx.astype(BF16)
        tail_ref[m] = dx[rows - 16 :]
        spill_ref[m] = spill


def output_kernel(me_ref, grad_ref, tail_ref, spill_ref, w_ref, o0, o1, o2, o3, lhs, fixed):
    rows = grad_ref.shape[1]
    part = rows // 4

    @pl.when(pl.program_id(0) == 0)
    def _():
        fixed[...] = grad_ref[...]
        for m in range(3):
            add = jnp.concatenate([jnp.zeros((8, spill_ref.shape[2]), F32), spill_ref[m]], 0)
            fixed[m, rows - 16 :] = (tail_ref[m] + add).astype(BF16)
        for k in range(4):
            at = pl.multiple_of(lax.rem(me_ref[3] + k, 4) * part, part)
            for m in range(3):
                lhs[m, k * part : (k + 1) * part] = fixed[m, pl.ds(at, part)]

    total = dot(lhs[0], w_ref[0], NT) + dot(lhs[1], w_ref[1], NT) + dot(lhs[2], w_ref[2], NT)
    o0[...] = total[:part]
    for k, ref in ((1, o1), (2, o2), (3, o3)):
        ref[...] = total[k * part : (k + 1) * part].astype(BF16)


def on_device(inputs, projection, conv_weight, gate_code, beta_code, grad_out):
    n = lax.axis_size("ctx")
    heads = lax.axis_size("head")
    zs = n // (2 * XS)
    rows, width = inputs.shape
    lanes = projection.shape[2]
    blocks = rows // BLOCK
    at = lax.axis_index("ctx")
    me = jnp.stack([at % 2, (at // 2) % XS, at // (2 * XS), lax.axis_index("head")]).astype(
        jnp.int32
    )
    x_groups = [[(z * XS + x) * 2 + c for x in range(XS)] for z in range(zs) for c in range(2)]
    z_groups = [[(z * XS + x) * 2 + c for z in range(zs)] for x in range(XS) for c in range(2)]

    def swap(block, bit):
        return lax.ppermute(block, "ctx", [(i, i ^ bit) for i in range(n)])

    projected, tail = pl.pallas_call(
        project_kernel,
        grid=(3,),
        in_specs=[
            pl.BlockSpec((rows, width), lambda m: (0, 0)),
            pl.BlockSpec((1, width, lanes), lambda m: (m, 0, 0)),
        ],
        out_specs=(
            pl.BlockSpec((1, rows, lanes), lambda m: (m, 0, 0)),
            pl.BlockSpec((1, 8, lanes), lambda m: (m, 0, 0)),
        ),
        out_shape=(shape((3, rows, lanes), BF16), shape((3, 8, lanes))),
    )(inputs, projection)
    halo = lax.ppermute(tail, "ctx", [(i, i + 1) for i in range(n - 1)])
    square = (2, rows, rows)
    tall = (2, rows, DK)
    triple = (3, DK, DK)
    keep, send, z, q, k, w, u, p, d, a, t, col = call(
        local_kernel,
        (
            shape(triple), shape(triple), shape((3, rows, lanes)), shape(tall), shape(tall),
            shape(tall), shape(tall), shape(square), shape(square), shape(square),
            shape((2, blocks, BLOCK, BLOCK)), shape((2, 3, rows, DK)),
        ),
        scratch=(pltpu.VMEM((3, rows + 8, lanes), F32), pltpu.VMEM((2, 3, DK, DK), F32)),
        smem=1,
        flops=2_000_000_000,
    )(me, projected, halo, conv_weight, gate_code, beta_code, grad_out)
    recv = swap(send, 1)
    dr, e = call(adjoint_kernel, (shape(tall), shape(tall)), flops=500_000_000)(
        p, a, t, k, col, grad_out
    )
    xsend = call(pair_kernel, shape((XS, 3, DK, DK), BF16), smem=1)(me, keep, recv)
    xrecv = lax.all_to_all(xsend, "ctx", 0, 0, axis_index_groups=x_groups)
    pre, suf, zsend = call(
        group_kernel,
        (shape((2, DK, DK)), shape((2, DK, DK)), shape((zs, 2, DK, DK), BF16)),
        smem=1,
    )(me, xrecv)
    zrecv = lax.all_to_all(zsend, "ctx", 0, 0, axis_index_groups=z_groups)
    own, other = call(enter_kernel, (shape((2, DK, DK)), shape((2, DK, DK))), smem=1)(
        me, zrecv, pre, suf, keep, recv
    )
    other = swap(other, 1)
    rounded, edge, spill, taps = call(
        backward_kernel,
        (
            shape((3, rows, lanes), BF16), shape((3, 16, lanes)), shape((3, 8, lanes)),
            shape((3, KW, lanes)),
        ),
        scratch=(
            pltpu.VMEM((3, rows + 8, lanes), F32),
            pltpu.VMEM((3, rows + 16, lanes), F32),
        ),
        smem=1,
        flops=2_000_000_000,
    )(me, own, other, projected, halo, conv_weight, grad_out, z, q, k, w, u, d, col, dr, e)
    spill = lax.ppermute(spill, "ctx", [(i + 1, i) for i in range(n - 1)])
    part = rows // heads
    step = 512
    out = pl.BlockSpec((part, step), lambda i: (0, i))
    mine, *sends = pl.pallas_call(
        output_kernel,
        grid=(width // step,),
        in_specs=[
            pl.BlockSpec(memory_space=pltpu.SMEM),
            pl.BlockSpec((3, rows, lanes), lambda i: (0, 0, 0)),
            pl.BlockSpec((3, 16, lanes), lambda i: (0, 0, 0)),
            pl.BlockSpec((3, 8, lanes), lambda i: (0, 0, 0)),
            pl.BlockSpec((3, step, lanes), lambda i: (0, i, 0)),
        ],
        out_specs=(out,) * 4,
        out_shape=(shape((part, width)),) + (shape((part, width), BF16),) * 3,
        scratch_shapes=[pltpu.VMEM((3, rows, lanes), BF16)] * 2,
        cost_estimate=pl.CostEstimate(
            flops=2 * 3 * rows * lanes * width, bytes_accessed=4_000_000, transcendentals=0
        ),
    )(me, rounded, edge, spill, projection)
    total = mine
    for shift, block in enumerate(sends, 1):
        got = lax.ppermute(block, "head", [(i, (i + shift) % heads) for i in range(heads)])
        total = total + got.astype(F32)
    bit = 1
    while bit < n:
        taps = taps + swap(taps, bit)
        bit *= 2
    return (total.astype(BF16), taps)


def solution(mesh):
    return jax.shard_map(
        on_device,
        mesh=mesh,
        in_specs=(
            P("ctx", None),
            P(None, None, "head"),
            P(None, None, "head"),
            P("head", "ctx"),
            P("head", "ctx"),
            P("ctx", "head"),
        ),
        out_specs=(P(("ctx", "head"), None), P(None, None, "head")),
        check_vma=False,
    )
```

```python
import jax
import jax.numpy as jnp
from jax import lax
from jax.experimental import pallas as pl
from jax.experimental.pallas import tpu as pltpu
from jax.sharding import PartitionSpec as P


DK = 128
KW = 4
BLOCK = 64
XS = 4
LIMIT = 20 * 2**20
SCALE = DK**-0.5
F32 = jnp.float32
BF16 = jnp.bfloat16
HIGHEST = lax.Precision.HIGHEST
NN = (((1,), (0,)), ((), ()))
NT = (((1,), (1,)), ((), ()))
TN = (((0,), (0,)), ((), ()))


def split(a):
    high = a.astype(BF16)
    return high, (a - high.astype(F32)).astype(BF16)


def dot(a, b, dims):
    return lax.dot_general(a, b, dims, preferred_element_type=F32)


def mm(a, b, dims=NN):
    ah, al = split(a)
    bh, bl = split(b)
    return dot(ah, bh, dims) + (dot(ah, bl, dims) + dot(al, bh, dims))


def mm_left(a, b, dims=NN):
    ah, al = split(a)
    return dot(ah, b, dims) + dot(al, b, dims)


def mm_right(a, b, dims=NN):
    bh, bl = split(b)
    return dot(a, bh, dims) + dot(a, bl, dims)


def exact(a, b, dims):
    return lax.dot_general(a, b, dims, precision=HIGHEST, preferred_element_type=F32)


def iotas(rows, cols):
    return (
        lax.broadcasted_iota(jnp.int32, (rows, cols), 0),
        lax.broadcasted_iota(jnp.int32, (rows, cols), 1),
    )


def eye(n):
    r, c = iotas(n, n)
    return (r == c).astype(F32)


def call(kernel, out_shape, scratch=(), smem=0, flops=0, **kw):
    def run(*args):
        specs = [
            pl.BlockSpec(memory_space=pltpu.SMEM if i < smem else pltpu.VMEM)
            for i in range(len(args))
        ]
        return pl.pallas_call(
            kernel,
            out_shape=out_shape,
            in_specs=specs,
            out_specs=jax.tree.map(lambda _: pl.BlockSpec(memory_space=pltpu.VMEM), out_shape),
            scratch_shapes=list(scratch),
            cost_estimate=pl.CostEstimate(
                flops=flops, bytes_accessed=4_000_000, transcendentals=0
            ),
            compiler_params=pltpu.CompilerParams(vmem_limit_bytes=LIMIT),
            **kw,
        )(*args)

    return run


def shape(s, d=F32):
    return jax.ShapeDtypeStruct(s, d)


def project_kernel(x_ref, w_ref, o_ref, tail_ref):
    value = dot(x_ref[...], w_ref[0], NN).astype(BF16)
    o_ref[0] = value
    rows = value.shape[0]
    tail_ref[0] = value[rows - 16 :].astype(F32)[8:]


def sigmoid(z):
    return 1.0 / (1.0 + jnp.exp(-z))


def local_kernel(
    me_ref, proj_ref, halo_ref, cw_ref, gate_ref, beta_ref, grad_ref,
    keep_ref, send_ref, z_ref, q_ref, k_ref, w_ref, u_ref, p_ref, d_ref, a_ref, t_ref, col_ref,
    ext, buf,
):
    rows = proj_ref.shape[1]
    blocks = rows // BLOCK
    for m in range(3):
        ext[m, 0:8] = halo_ref[m]
        ext[m, 8 : 8 + rows] = proj_ref[m].astype(F32)
    act = []
    for m in range(3):
        z = cw_ref[m, 0:1] * ext[m, 5 : 5 + rows]
        for j in range(1, KW):
            z = z + cw_ref[m, j : j + 1] * ext[m, 5 + j : 5 + j + rows]
        z_ref[m] = z
        act.append(z * sigmoid(z))
    logs = jnp.log(1.0 - 0.001 * gate_ref[...].astype(F32) / 1023.0)
    beta = beta_ref[...].astype(F32) / 1023.0
    r, c = iotas(rows, rows)
    tri = (r >= c).astype(F32)
    col = exact(tri, logs, NT)
    row = exact(logs, tri, NT)
    betas = exact((r == c).astype(F32), beta, NT)
    r64, c64 = iotas(BLOCK, BLOCK)
    diag = []
    keys = []
    queries = []
    for h in range(2):
        lanes = slice(h * DK, (h + 1) * DK)
        aq = act[0][:, lanes]
        ak = act[1][:, lanes]
        queries.append(aq * lax.rsqrt(jnp.sum(aq * aq, -1, keepdims=True) + 1e-06) * SCALE)
        keys.append(ak * lax.rsqrt(jnp.sum(ak * ak, -1, keepdims=True) + 1e-06))
        b = col[:, h : h + 1]
        bt = betas[:, h : h + 1]
        decay = jnp.where(r >= c, jnp.exp(b - row[h : h + 1]), 0.0)
        d_ref[h] = decay
        gram = mm(keys[h], keys[h], NT)
        a_ref[h] = jnp.where(r > c, decay * gram * bt, 0.0)
        p_ref[h] = decay * mm(queries[h], keys[h], NT)
        q_ref[h] = queries[h]
        k_ref[h] = keys[h]
        total = col[rows - 1 : rows, h : h + 1]
        col_ref[h, 0] = jnp.broadcast_to(jnp.exp(b), (rows, DK))
        col_ref[h, 1] = jnp.broadcast_to(bt, (rows, DK))
        col_ref[h, 2] = jnp.broadcast_to(jnp.exp(total - b), (rows, DK))
        for i in range(blocks):
            span = slice(i * BLOCK, (i + 1) * BLOCK)
            kb = keys[h][span]
            rb = exact(logs, tri[span], NT)[h : h + 1]
            dec = jnp.exp(b[span] - rb)
            diag.append(jnp.where(r64 > c64, dec * mm(kb, kb, NT) * bt[span], 0.0))
    lower = jnp.stack(diag)
    count = len(diag)
    tiles = []
    for k in range(BLOCK // 8):
        rr = lax.broadcasted_iota(jnp.int32, (count, 8, BLOCK), 1) + 8 * k
        cc = lax.broadcasted_iota(jnp.int32, (count, 8, BLOCK), 2)
        tiles.append((rr == cc).astype(F32))
    for s in range(BLOCK - 1):
        k0, r0 = divmod(s, 8)
        pivot = tiles[k0][:, r0 : r0 + 1, :]
        for k in range(k0, BLOCK // 8):
            tiles[k] = tiles[k] - lower[:, 8 * k : 8 * k + 8, s : s + 1] * pivot
    inverse = jnp.concatenate(tiles, 1)
    for h in range(2):
        for i in range(blocks):
            t_ref[h, i] = inverse[h * blocks + i]
    for h in range(2):
        lanes = slice(h * DK, (h + 1) * DK)
        eb = col_ref[h, 0]
        bt = col_ref[h, 1]
        rest = col_ref[h, 2]
        rhs = jnp.concatenate([bt * eb * keys[h], bt * act[2][:, lanes]], 1)
        done = []
        for i in range(blocks):
            span = slice(i * BLOCK, (i + 1) * BLOCK)
            part = rhs[span]
            if i > 0:
                past = jnp.concatenate(done, 0) if i > 1 else done[0]
                part = part - mm(a_ref[h, span, 0 : i * BLOCK], past)
            done.append(mm(inverse[h * blocks + i], part))
        wu = jnp.concatenate(done, 0)
        w = wu[:, :DK]
        w_ref[h] = w
        u_ref[h] = wu[:, DK:]
        kt = rest * keys[h]
        ml = mm(wu, kt, TN)
        buf[h, 0] = eb[rows - 1 : rows] * eye(DK) - ml[:DK]
        buf[h, 1] = ml[DK:]
        effective = eb * queries[h] - mm(p_ref[h], w)
        buf[h, 2] = mm_right(grad_ref[:, lanes], effective, TN)
    core = me_ref[0]
    keep_ref[...] = buf[core]
    send_ref[...] = buf[1 - core]


def adjoint_kernel(p_ref, a_ref, t_ref, k_ref, col_ref, grad_ref, dr_ref, e_ref):
    rows = k_ref.shape[1]
    blocks = rows // BLOCK
    for h in range(2):
        lanes = slice(h * DK, (h + 1) * DK)
        back = mm_left(p_ref[h], grad_ref[:, lanes], TN)
        rhs = jnp.concatenate([back, col_ref[h, 2] * k_ref[h]], 1)
        done = {}
        for i in reversed(range(blocks)):
            span = slice(i * BLOCK, (i + 1) * BLOCK)
            part = rhs[span]
            for j in range(i + 1, blocks):
                below = slice(j * BLOCK, (j + 1) * BLOCK)
                wide = mm(a_ref[h, below], done[j], TN)
                part = part - wide[span]
            done[i] = mm(t_ref[h, i], part, TN)
        full = jnp.concatenate([done[i] for i in range(blocks)], 0)
        dr_ref[h] = full[:, :DK]
        e_ref[h] = full[:, DK:]


def ordered_pair(me_ref, keep_ref, recv_ref):
    first = me_ref[0] == 0
    keep, recv = keep_ref[...], recv_ref[...]
    return jnp.where(first, keep, recv), jnp.where(first, recv, keep)


def pair_kernel(me_ref, keep_ref, recv_ref, out_ref):
    e0, e1 = ordered_pair(me_ref, keep_ref, recv_ref)
    both = mm(jnp.concatenate([e0[0], e0[1]], 0), e1[0])
    out_ref[0] = (both[:DK] - eye(DK)).astype(BF16)
    out_ref[1] = (both[DK:] + e1[1]).astype(BF16)
    out_ref[2] = (mm(e1[2], e0[0], NT) + e0[2]).astype(BF16)


def group_kernel(me_ref, own_ref, r1, r2, r3, pre_ref, suf_ref, out_ref, el):
    x = me_ref[1]
    one = eye(DK)
    zero = jnp.zeros((DK, DK), F32)
    for k, ref in enumerate((own_ref, r1, r2, r3)):
        el[lax.rem(x + XS - k, XS)] = ref[...]

    def put(ref, value):
        ref[0] = value[:DK]
        ref[1] = value[DK:]

    start = jnp.concatenate([one, zero], 0)
    fwd = start
    bwd = start
    for j in range(XS):

        @pl.when(x == j)
        def _(fwd=fwd):
            put(pre_ref, fwd)

        @pl.when(x == XS - 1 - j)
        def _(bwd=bwd):
            put(suf_ref, bwd)

        mf = el[j, 0]
        mb = el[XS - 1 - j, 0]
        lf = el[j, 1].astype(F32)
        gb = el[XS - 1 - j, 2].astype(F32)
        if j == 0:
            fwd = jnp.concatenate([one + mf.astype(F32), lf], 0)
            bwd = jnp.concatenate([one + mb.astype(F32).T, gb], 0)
        else:
            fwd = fwd + mm_left(fwd, mf, NN) + jnp.concatenate([zero, lf], 0)
            bwd = bwd + mm_left(bwd, mb, NT) + jnp.concatenate([zero, gb], 0)
    out_ref[0] = (fwd[:DK] - one).astype(BF16)
    out_ref[1] = fwd[DK:].astype(BF16)
    out_ref[2] = bwd[DK:].astype(BF16)


def merge_kernel(me_ref, own_ref, recv_ref, o1, o2, o3):
    first = lax.rem(me_ref[2], 2) == 0
    pair = me_ref[2] // 2
    own, recv = own_ref[...], recv_ref[...]
    e0 = jnp.where(first, own, recv)
    e1 = jnp.where(first, recv, own)
    both = dot(jnp.concatenate([e0[0], e0[1]], 0), e1[0], NN)
    m = e0[0].astype(F32) + e1[0].astype(F32) + both[:DK]
    s = e0[1].astype(F32) + e1[1].astype(F32) + both[DK:]
    g = e0[2].astype(F32) + e1[2].astype(F32) + dot(e1[2], e0[0], NT)
    m = m.astype(BF16)
    for k, ref in ((1, o1), (2, o2), (3, o3)):
        ref[0] = m
        ref[1] = jnp.where(pair + k < 4, s, g).astype(BF16)


def enter_kernel(
    me_ref, r1, r2, r3, near_ref, pre_ref, suf_ref, keep_ref, recv_ref, own_ref, send_ref
):
    z = me_ref[2]
    pair = z // 2
    first = lax.rem(z, 2) == 0
    s = jnp.zeros((DK, DK), F32)
    g = jnp.zeros((DK, DK), F32)
    for k, ref in ((3, r3), (2, r2), (1, r1)):
        add = ref[1].astype(F32)
        new = add if k == 3 else s + mm_left(s, ref[0], NN) + add
        s = jnp.where(k <= pair, new, s)
    for k, ref in ((1, r1), (2, r2), (3, r3)):
        add = ref[1].astype(F32)
        new = add if k == 1 else g + mm_left(g, ref[0], NT) + add
        g = jnp.where(k > pair, new, g)
    near = near_ref[0]
    s = jnp.where(first, s, s + mm_left(s, near, NN) + near_ref[1].astype(F32))
    g = jnp.where(first, g + mm_left(g, near, NT) + near_ref[2].astype(F32), g)
    s = mm(s, pre_ref[0]) + pre_ref[1]
    g = mm(g, suf_ref[0]) + suf_ref[1]
    e0, e1 = ordered_pair(me_ref, keep_ref, recv_ref)
    s1 = mm(s, e0[0]) + e0[1]
    g0 = mm(g, e1[0], NT) + e1[2]
    first = me_ref[0] == 0
    own_ref[0] = jnp.where(first, s, s1)
    own_ref[1] = jnp.where(first, g0, g)
    send_ref[0] = jnp.where(first, s1, s)
    send_ref[1] = jnp.where(first, g, g0)


def backward_kernel(
    me_ref, own_ref, recv_ref, proj_ref, halo_ref, cw_ref, grad_ref,
    z_ref, q_ref, k_ref, w_ref, u_ref, d_ref, col_ref, dr_ref, e_ref,
    out_ref, tail_ref, spill_ref, taps_ref,
    ext, dzs,
):
    rows = proj_ref.shape[1]
    core = me_ref[0]
    r, c = iotas(rows, rows)
    pads = jnp.zeros((8, dzs.shape[2]), F32)
    for m in range(3):
        ext[m, 0:8] = halo_ref[m]
        ext[m, 8 : 8 + rows] = proj_ref[m].astype(F32)
        dzs[m, 0:8] = pads
        dzs[m, 8 + rows : 16 + rows] = pads
    for h in range(2):
        lanes = slice(h * DK, (h + 1) * DK)
        mine = core == h
        s = jnp.where(mine, own_ref[0], recv_ref[0])
        g = jnp.where(mine, own_ref[1], recv_ref[1])
        q, k = q_ref[h], k_ref[h]
        eb, bt, rest = col_ref[h, 0], col_ref[h, 1], col_ref[h, 2]
        do = grad_ref[:, lanes].astype(F32)
        u = u_ref[h] - mm(w_ref[h], s, NT)
        dr = dr_ref[h] + mm(e_ref[h], g, NT)
        cross = mm(jnp.concatenate([do, dr], 0), u, NT)
        decay = d_ref[h]
        x1 = decay * cross[:rows]
        da = jnp.where(r > c, decay * cross[rows:], 0.0) * -bt[:, :1]
        outer = mm(jnp.concatenate([eb * do, -(bt * eb) * dr], 0), s)
        right = mm(jnp.concatenate([x1, da], 0), k)
        dq = outer[:rows] + right[:rows]
        dk = outer[rows:] + right[rows:] + rest * mm(u, g)
        dk = dk + mm(jnp.concatenate([x1, da], 0), jnp.concatenate([q, k], 0), TN)
        dv = bt * dr
        zq = z_ref[0, :, lanes]
        zk = z_ref[1, :, lanes]
        zv = z_ref[2, :, lanes]
        sq, sk, sv = sigmoid(zq), sigmoid(zk), sigmoid(zv)
        aq, ak = zq * sq, zk * sk
        rq = lax.rsqrt(jnp.sum(aq * aq, -1, keepdims=True) + 1e-06)
        rk = lax.rsqrt(jnp.sum(ak * ak, -1, keepdims=True) + 1e-06)
        daq = rq * (SCALE * dq - q * (jnp.sum(q * dq, -1, keepdims=True) * (1.0 / SCALE)))
        dak = rk * (dk - k * jnp.sum(k * dk, -1, keepdims=True))
        dzs[0, 8 : 8 + rows, lanes] = daq * (sq * (1.0 + zq * (1.0 - sq)))
        dzs[1, 8 : 8 + rows, lanes] = dak * (sk * (1.0 + zk * (1.0 - sk)))
        dzs[2, 8 : 8 + rows, lanes] = dv * (sv * (1.0 + zv * (1.0 - sv)))
    for m in range(3):
        dz = dzs[m, 8 : 8 + rows]
        dx = None
        spill = None
        for j in range(KW):
            tap = cw_ref[m, j : j + 1]
            term = tap * dzs[m, 11 - j : 11 - j + rows]
            first = tap * dzs[m, 3 - j : 11 - j]
            dx = term if dx is None else dx + term
            spill = first if spill is None else spill + first
            taps_ref[m, j : j + 1] = jnp.sum(dz * ext[m, 5 + j : 5 + j + rows], 0, keepdims=True)
        out_ref[m] = dx.astype(BF16)
        tail_ref[m] = dx[rows - 16 :]
        spill_ref[m] = spill


def output_kernel(me_ref, grad_ref, tail_ref, spill_ref, w_ref, o0, o1, o2, o3, lhs, fixed):
    rows = grad_ref.shape[1]
    part = rows // 4

    @pl.when(pl.program_id(0) == 0)
    def _():
        fixed[...] = grad_ref[...]
        for m in range(3):
            add = jnp.concatenate([jnp.zeros((8, spill_ref.shape[2]), F32), spill_ref[m]], 0)
            fixed[m, rows - 16 :] = (tail_ref[m] + add).astype(BF16)
        for k in range(4):
            at = pl.multiple_of(lax.rem(me_ref[3] + k, 4) * part, part)
            for m in range(3):
                lhs[m, k * part : (k + 1) * part] = fixed[m, pl.ds(at, part)]

    total = dot(lhs[0], w_ref[0], NT) + dot(lhs[1], w_ref[1], NT) + dot(lhs[2], w_ref[2], NT)
    o0[...] = total[:part]
    for k, ref in ((1, o1), (2, o2), (3, o3)):
        ref[...] = total[k * part : (k + 1) * part].astype(BF16)


def body(inputs, projection, conv_weight, gate_code, beta_code, grad_out):
    n = lax.axis_size("ctx")
    heads = lax.axis_size("head")
    rows, width = inputs.shape
    lanes = projection.shape[2]
    blocks = rows // BLOCK
    at = lax.axis_index("ctx")
    me = jnp.stack([at % 2, (at // 2) % XS, at // (2 * XS), lax.axis_index("head")]).astype(
        jnp.int32
    )

    def swap(block, bit):
        return lax.ppermute(block, "ctx", [(i, i ^ bit) for i in range(n)])

    def turn(block, stride, k):
        route = []
        for i in range(n):
            place = (i // stride) % 4
            route.append((i, i + ((place + k) % 4 - place) * stride))
        return lax.ppermute(block, "ctx", route)


    projected, tail = pl.pallas_call(
        project_kernel,
        grid=(3,),
        in_specs=[
            pl.BlockSpec((rows, width), lambda m: (0, 0)),
            pl.BlockSpec((1, width, lanes), lambda m: (m, 0, 0)),
        ],
        out_specs=(
            pl.BlockSpec((1, rows, lanes), lambda m: (m, 0, 0)),
            pl.BlockSpec((1, 8, lanes), lambda m: (m, 0, 0)),
        ),
        out_shape=(shape((3, rows, lanes), BF16), shape((3, 8, lanes))),
        compiler_params=pltpu.CompilerParams(vmem_limit_bytes=LIMIT),
    )(inputs, projection)
    halo = lax.ppermute(tail, "ctx", [(i, i + 1) for i in range(n - 1)])
    square = (2, rows, rows)
    tall = (2, rows, DK)
    triple = (3, DK, DK)
    keep, send, z, q, k, w, u, p, d, a, t, col = call(
        local_kernel,
        (
            shape(triple), shape(triple), shape((3, rows, lanes)), shape(tall), shape(tall),
            shape(tall), shape(tall), shape(square), shape(square), shape(square),
            shape((2, blocks, BLOCK, BLOCK)), shape((2, 3, rows, DK)),
        ),
        scratch=(pltpu.VMEM((3, rows + 8, lanes), F32), pltpu.VMEM((2, 3, DK, DK), F32)),
        smem=1,
        flops=2_000_000_000,
    )(me, projected, halo, conv_weight, gate_code, beta_code, grad_out)
    recv = swap(send, 1)
    dr, e = call(adjoint_kernel, (shape(tall), shape(tall)), flops=500_000_000)(
        p, a, t, k, col, grad_out
    )
    group = call(pair_kernel, shape(triple, BF16), smem=1)(me, keep, recv)
    pre, suf, whole = call(
        group_kernel,
        (shape((2, DK, DK)), shape((2, DK, DK)), shape(triple, BF16)),
        scratch=(pltpu.VMEM((XS, 3, DK, DK), BF16),),
        smem=1,
    )(me, group, *(turn(group, 2, k) for k in (1, 2, 3)))
    near = swap(whole, 2 * XS)
    far = call(merge_kernel, (shape((2, DK, DK), BF16),) * 3, smem=1)(me, whole, near)
    far = [turn(block, 4 * XS, k) for k, block in enumerate(far, 1)]
    own, other = call(enter_kernel, (shape((2, DK, DK)), shape((2, DK, DK))), smem=1)(
        me, *far, near, pre, suf, keep, recv
    )
    other = swap(other, 1)
    rounded, edge, spill, taps = call(
        backward_kernel,
        (
            shape((3, rows, lanes), BF16), shape((3, 16, lanes)), shape((3, 8, lanes)),
            shape((3, KW, lanes)),
        ),
        scratch=(
            pltpu.VMEM((3, rows + 8, lanes), F32),
            pltpu.VMEM((3, rows + 16, lanes), F32),
        ),
        smem=1,
        flops=2_000_000_000,
    )(me, own, other, projected, halo, conv_weight, grad_out, z, q, k, w, u, d, col, dr, e)
    spill = lax.ppermute(spill, "ctx", [(i + 1, i) for i in range(n - 1)])
    part = rows // heads
    step = 512
    out = pl.BlockSpec((part, step), lambda i: (0, i))
    mine, *sends = pl.pallas_call(
        output_kernel,
        grid=(width // step,),
        in_specs=[
            pl.BlockSpec(memory_space=pltpu.SMEM),
            pl.BlockSpec((3, rows, lanes), lambda i: (0, 0, 0)),
            pl.BlockSpec((3, 16, lanes), lambda i: (0, 0, 0)),
            pl.BlockSpec((3, 8, lanes), lambda i: (0, 0, 0)),
            pl.BlockSpec((3, step, lanes), lambda i: (0, i, 0)),
        ],
        out_specs=(out,) * 4,
        out_shape=(shape((part, width)),) + (shape((part, width), BF16),) * 3,
        scratch_shapes=[pltpu.VMEM((3, rows, lanes), BF16)] * 2,
        compiler_params=pltpu.CompilerParams(vmem_limit_bytes=LIMIT),
        cost_estimate=pl.CostEstimate(
            flops=2 * 3 * rows * lanes * width, bytes_accessed=4_000_000, transcendentals=0
        ),
    )(me, rounded, edge, spill, projection)
    total = mine
    for shift, block in enumerate(sends, 1):
        got = lax.ppermute(block, "head", [(i, (i + shift) % heads) for i in range(heads)])
        total = total + got.astype(F32)

    def around(taps, stride):
        r1, r2, r3 = (turn(taps, stride, k) for k in (1, 2, 3))
        return (taps + r2) + (r1 + r3)

    taps = taps + swap(taps, 1)
    taps = around(taps, 2)
    taps = taps + swap(taps, 2 * XS)
    taps = around(taps, 4 * XS)
    return (total.astype(BF16), taps)


def solution(mesh):
    return jax.shard_map(
        body,
        mesh=mesh,
        in_specs=(
            P("ctx", None),
            P(None, None, "head"),
            P(None, None, "head"),
            P("head", "ctx"),
            P("head", "ctx"),
            P("ctx", "head"),
        ),
        out_specs=(P(("ctx", "head"), None), P(None, None, "head")),
        check_vma=False,
    )
```

```python
import jax
import jax.numpy as jnp
from jax import lax
from jax.experimental import pallas as pl
from jax.experimental.pallas import tpu as pltpu
from jax.sharding import PartitionSpec as P


DK = 128
KW = 4
BLOCK = 64
XS = 4
LIMIT = 20 * 2**20
SCALE = DK**-0.5
F32 = jnp.float32
BF16 = jnp.bfloat16
NN = (((1,), (0,)), ((), ()))
NT = (((1,), (1,)), ((), ()))
TN = (((0,), (0,)), ((), ()))


def split(a):
    high = a.astype(BF16)
    return high, (a - high.astype(F32)).astype(BF16)


def dot(a, b, dims):
    return lax.dot_general(a, b, dims, preferred_element_type=F32)


def mm(a, b, dims=NN):
    ah, al = split(a)
    bh, bl = split(b)
    return dot(ah, bh, dims) + (dot(ah, bl, dims) + dot(al, bh, dims))


def mm_left(a, b, dims=NN):
    ah, al = split(a)
    return dot(ah, b, dims) + dot(al, b, dims)


def mm_right(a, b, dims=NN):
    bh, bl = split(b)
    return dot(a, bh, dims) + dot(a, bl, dims)


def pieces(a):
    high, low = split(a)
    return high, low, (a - high.astype(F32) - low.astype(F32)).astype(BF16)


def iotas(rows, cols):
    return (
        lax.broadcasted_iota(jnp.int32, (rows, cols), 0),
        lax.broadcasted_iota(jnp.int32, (rows, cols), 1),
    )


def eye(n):
    r, c = iotas(n, n)
    return (r == c).astype(F32)


def call(kernel, out_shape, scratch=(), smem=0, flops=0, **kw):
    def run(*args):
        specs = [
            pl.BlockSpec(memory_space=pltpu.SMEM if i < smem else pltpu.VMEM)
            for i in range(len(args))
        ]
        return pl.pallas_call(
            kernel,
            out_shape=out_shape,
            in_specs=specs,
            out_specs=jax.tree.map(lambda _: pl.BlockSpec(memory_space=pltpu.VMEM), out_shape),
            scratch_shapes=list(scratch),
            cost_estimate=pl.CostEstimate(
                flops=flops, bytes_accessed=4_000_000, transcendentals=0
            ),
            compiler_params=pltpu.CompilerParams(vmem_limit_bytes=LIMIT),
            **kw,
        )(*args)

    return run


def shape(s, d=F32):
    return jax.ShapeDtypeStruct(s, d)


def project_kernel(x_ref, w_ref, o_ref, tail_ref, x_held, w_held, sems):
    copies = [pltpu.make_async_copy(x_ref, x_held, sems.at[3])]
    for m in range(3):
        copies.append(pltpu.make_async_copy(w_ref.at[m], w_held.at[m], sems.at[m]))
    for copy in copies:
        copy.start()
    copies[0].wait()
    rows = x_ref.shape[0]
    for m in range(3):
        copies[1 + m].wait()
        value = dot(x_held[...], w_held[m], NN).astype(BF16)
        o_ref[m] = value
        tail_ref[m] = value[rows - 16 :].astype(F32)[8:]


def sigmoid(z):
    return 1.0 / (1.0 + jnp.exp(-z))


def local_kernel(
    me_ref, proj_ref, halo_ref, cw_ref, gate_ref, beta_ref, grad_ref,
    keep_ref, send_ref, z_ref, q_ref, k_ref, w_ref, u_ref, p_ref, d_ref, a_ref, t_ref, col_ref,
    ext, buf,
):
    rows = proj_ref.shape[1]
    blocks = rows // BLOCK
    for m in range(3):
        ext[m, 0:8] = halo_ref[m]
        ext[m, 8 : 8 + rows] = proj_ref[m].astype(F32)
    act = []
    for m in range(3):
        z = cw_ref[m, 0:1] * ext[m, 5 : 5 + rows]
        for j in range(1, KW):
            z = z + cw_ref[m, j : j + 1] * ext[m, 5 + j : 5 + j + rows]
        z_ref[m] = z
        act.append(z * sigmoid(z))
    logs = jnp.log(1.0 - 0.001 * gate_ref[...].astype(F32) / 1023.0)
    beta = beta_ref[...].astype(F32) / 1023.0
    r, c = iotas(rows, rows)
    tri = jnp.where(r >= c, 1.0, 0.0).astype(BF16)
    unit = jnp.where(r == c, 1.0, 0.0).astype(BF16)
    col = sum(dot(tri, piece, NT) for piece in pieces(logs))
    row = sum(dot(piece, tri, NT) for piece in pieces(logs))
    betas = sum(dot(unit, piece, NT) for piece in pieces(beta))
    diag = []
    keys = []
    queries = []
    for h in range(2):
        lanes = slice(h * DK, (h + 1) * DK)
        aq = act[0][:, lanes]
        ak = act[1][:, lanes]
        queries.append(aq * lax.rsqrt(jnp.sum(aq * aq, -1, keepdims=True) + 1e-06) * SCALE)
        keys.append(ak * lax.rsqrt(jnp.sum(ak * ak, -1, keepdims=True) + 1e-06))
        b = col[:, h : h + 1]
        bt = betas[:, h : h + 1]
        decay = jnp.where(r >= c, jnp.exp(b - row[h : h + 1]), 0.0)
        d_ref[h] = decay
        gram = mm(keys[h], keys[h], NT)
        low = jnp.where(r > c, decay * gram * bt, 0.0)
        a_ref[h] = low
        p_ref[h] = decay * mm(queries[h], keys[h], NT)
        q_ref[h] = queries[h]
        k_ref[h] = keys[h]
        total = col[rows - 1 : rows, h : h + 1]
        col_ref[h, 0] = jnp.broadcast_to(jnp.exp(b), (rows, DK))
        col_ref[h, 1] = jnp.broadcast_to(bt, (rows, DK))
        col_ref[h, 2] = jnp.broadcast_to(jnp.exp(total - b), (rows, DK))
        for i in range(blocks):
            span = slice(i * BLOCK, (i + 1) * BLOCK)
            diag.append(low[span, span])
    lower = jnp.stack(diag)
    count = len(diag)
    tiles = []
    for k in range(BLOCK // 8):
        rr = lax.broadcasted_iota(jnp.int32, (count, 8, BLOCK), 1) + 8 * k
        cc = lax.broadcasted_iota(jnp.int32, (count, 8, BLOCK), 2)
        tiles.append((rr == cc).astype(F32))
    for s in range(BLOCK - 1):
        k0, r0 = divmod(s, 8)
        pivot = tiles[k0][:, r0 : r0 + 1, :]
        for k in range(k0, BLOCK // 8):
            tiles[k] = tiles[k] - lower[:, 8 * k : 8 * k + 8, s : s + 1] * pivot
    inverse = jnp.concatenate(tiles, 1)
    for h in range(2):
        for i in range(blocks):
            t_ref[h, i] = inverse[h * blocks + i]
    for h in range(2):
        lanes = slice(h * DK, (h + 1) * DK)
        eb = col_ref[h, 0]
        bt = col_ref[h, 1]
        rest = col_ref[h, 2]
        rhs = jnp.concatenate([bt * eb * keys[h], bt * act[2][:, lanes]], 1)
        done = []
        for i in range(blocks):
            span = slice(i * BLOCK, (i + 1) * BLOCK)
            part = rhs[span]
            if i > 0:
                past = jnp.concatenate(done, 0) if i > 1 else done[0]
                part = part - mm(a_ref[h, span, 0 : i * BLOCK], past)
            done.append(mm(inverse[h * blocks + i], part))
        wu = jnp.concatenate(done, 0)
        w = wu[:, :DK]
        w_ref[h] = w
        u_ref[h] = wu[:, DK:]
        kt = rest * keys[h]
        ml = mm(wu, kt, TN)
        buf[h, 0] = eb[rows - 1 : rows] * eye(DK) - ml[:DK]
        buf[h, 1] = ml[DK:]
        effective = eb * queries[h] - mm(p_ref[h], w)
        buf[h, 2] = mm_right(grad_ref[:, lanes], effective, TN)
    core = me_ref[0]
    keep_ref[...] = buf[core]
    send_ref[...] = buf[1 - core]


def adjoint_kernel(p_ref, a_ref, t_ref, k_ref, col_ref, grad_ref, dr_ref, e_ref):
    rows = k_ref.shape[1]
    blocks = rows // BLOCK
    for h in range(2):
        lanes = slice(h * DK, (h + 1) * DK)
        back = mm_left(p_ref[h], grad_ref[:, lanes], TN)
        rhs = jnp.concatenate([back, col_ref[h, 2] * k_ref[h]], 1)
        done = {}
        for i in reversed(range(blocks)):
            span = slice(i * BLOCK, (i + 1) * BLOCK)
            part = rhs[span]
            for j in range(i + 1, blocks):
                below = slice(j * BLOCK, (j + 1) * BLOCK)
                wide = mm(a_ref[h, below], done[j], TN)
                part = part - wide[span]
            done[i] = mm(t_ref[h, i], part, TN)
        full = jnp.concatenate([done[i] for i in range(blocks)], 0)
        dr_ref[h] = full[:, :DK]
        e_ref[h] = full[:, DK:]


def ordered_pair(me_ref, keep_ref, recv_ref):
    first = me_ref[0] == 0
    keep, recv = keep_ref[...], recv_ref[...]
    return jnp.where(first, keep, recv), jnp.where(first, recv, keep)


def pair_kernel(me_ref, keep_ref, recv_ref, out_ref):
    e0, e1 = ordered_pair(me_ref, keep_ref, recv_ref)
    both = mm(jnp.concatenate([e0[0], e0[1]], 0), e1[0])
    out_ref[0] = (both[:DK] - eye(DK)).astype(BF16)
    out_ref[1] = (both[DK:] + e1[1]).astype(BF16)
    out_ref[2] = (mm(e1[2], e0[0], NT) + e0[2]).astype(BF16)


def group_kernel(me_ref, own_ref, r1, r2, r3, pre_ref, suf_ref, out_ref, el):
    x = me_ref[1]
    one = eye(DK)
    zero = jnp.zeros((DK, DK), F32)
    for k, ref in enumerate((own_ref, r1, r2, r3)):
        el[lax.rem(x + XS - k, XS)] = ref[...]

    def put(ref, value):
        ref[0] = value[:DK]
        ref[1] = value[DK:]

    start = jnp.concatenate([one, zero], 0)
    fwd = start
    bwd = start
    for j in range(XS):

        @pl.when(x == j)
        def _(fwd=fwd):
            put(pre_ref, fwd)

        @pl.when(x == XS - 1 - j)
        def _(bwd=bwd):
            put(suf_ref, bwd)

        mf = el[j, 0]
        mb = el[XS - 1 - j, 0]
        lf = el[j, 1].astype(F32)
        gb = el[XS - 1 - j, 2].astype(F32)
        if j == 0:
            fwd = jnp.concatenate([one + mf.astype(F32), lf], 0)
            bwd = jnp.concatenate([one + mb.astype(F32).T, gb], 0)
        else:
            fwd = fwd + mm_left(fwd, mf, NN) + jnp.concatenate([zero, lf], 0)
            bwd = bwd + mm_left(bwd, mb, NT) + jnp.concatenate([zero, gb], 0)
    out_ref[0] = (fwd[:DK] - one).astype(BF16)
    out_ref[1] = fwd[DK:].astype(BF16)
    out_ref[2] = bwd[DK:].astype(BF16)


def merge_kernel(me_ref, own_ref, recv_ref, o1, o2, o3):
    first = lax.rem(me_ref[2], 2) == 0
    pair = me_ref[2] // 2
    own, recv = own_ref[...], recv_ref[...]
    e0 = jnp.where(first, own, recv)
    e1 = jnp.where(first, recv, own)
    both = dot(jnp.concatenate([e0[0], e0[1]], 0), e1[0], NN)
    m = e0[0].astype(F32) + e1[0].astype(F32) + both[:DK]
    s = e0[1].astype(F32) + e1[1].astype(F32) + both[DK:]
    g = e0[2].astype(F32) + e1[2].astype(F32) + dot(e1[2], e0[0], NT)
    m = m.astype(BF16)
    for k, ref in ((1, o1), (2, o2), (3, o3)):
        ref[0] = m
        ref[1] = jnp.where(pair + k < 4, s, g).astype(BF16)


def enter_kernel(
    me_ref, r1, r2, r3, near_ref, pre_ref, suf_ref, keep_ref, recv_ref, own_ref, send_ref
):
    z = me_ref[2]
    pair = z // 2
    first = lax.rem(z, 2) == 0
    s = jnp.zeros((DK, DK), F32)
    g = jnp.zeros((DK, DK), F32)
    for k, ref in ((3, r3), (2, r2), (1, r1)):
        add = ref[1].astype(F32)
        new = add if k == 3 else s + mm_left(s, ref[0], NN) + add
        s = jnp.where(k <= pair, new, s)
    for k, ref in ((1, r1), (2, r2), (3, r3)):
        add = ref[1].astype(F32)
        new = add if k == 1 else g + mm_left(g, ref[0], NT) + add
        g = jnp.where(k > pair, new, g)
    near = near_ref[0]
    s = jnp.where(first, s, s + mm_left(s, near, NN) + near_ref[1].astype(F32))
    g = jnp.where(first, g + mm_left(g, near, NT) + near_ref[2].astype(F32), g)
    s = mm(s, pre_ref[0]) + pre_ref[1]
    g = mm(g, suf_ref[0]) + suf_ref[1]
    e0, e1 = ordered_pair(me_ref, keep_ref, recv_ref)
    s1 = mm(s, e0[0]) + e0[1]
    g0 = mm(g, e1[0], NT) + e1[2]
    first = me_ref[0] == 0
    own_ref[0] = jnp.where(first, s, s1)
    own_ref[1] = jnp.where(first, g0, g)
    send_ref[0] = jnp.where(first, s1, s)
    send_ref[1] = jnp.where(first, g, g0)


def backward_kernel(
    me_ref, own_ref, recv_ref, proj_ref, halo_ref, cw_ref, grad_ref,
    z_ref, q_ref, k_ref, w_ref, u_ref, d_ref, col_ref, dr_ref, e_ref,
    out_ref, tail_ref, spill_ref, taps_ref,
    ext, dzs,
):
    rows = proj_ref.shape[1]
    core = me_ref[0]
    r, c = iotas(rows, rows)
    pads = jnp.zeros((8, dzs.shape[2]), F32)
    for m in range(3):
        ext[m, 0:8] = halo_ref[m]
        ext[m, 8 : 8 + rows] = proj_ref[m].astype(F32)
        dzs[m, 0:8] = pads
        dzs[m, 8 + rows : 16 + rows] = pads
    for h in range(2):
        lanes = slice(h * DK, (h + 1) * DK)
        mine = core == h
        s = jnp.where(mine, own_ref[0], recv_ref[0])
        g = jnp.where(mine, own_ref[1], recv_ref[1])
        q, k = q_ref[h], k_ref[h]
        eb, bt, rest = col_ref[h, 0], col_ref[h, 1], col_ref[h, 2]
        do = grad_ref[:, lanes].astype(F32)
        u = u_ref[h] - mm(w_ref[h], s, NT)
        dr = dr_ref[h] + mm(e_ref[h], g, NT)
        cross = mm(jnp.concatenate([do, dr], 0), u, NT)
        decay = d_ref[h]
        x1 = decay * cross[:rows]
        da = jnp.where(r > c, decay * cross[rows:], 0.0) * -bt[:, :1]
        outer = mm(jnp.concatenate([eb * do, -(bt * eb) * dr], 0), s)
        right = mm(jnp.concatenate([x1, da], 0), k)
        dq = outer[:rows] + right[:rows]
        dk = outer[rows:] + right[rows:] + rest * mm(u, g)
        dk = dk + mm(jnp.concatenate([x1, da], 0), jnp.concatenate([q, k], 0), TN)
        dv = bt * dr
        zq = z_ref[0, :, lanes]
        zk = z_ref[1, :, lanes]
        zv = z_ref[2, :, lanes]
        sq, sk, sv = sigmoid(zq), sigmoid(zk), sigmoid(zv)
        aq, ak = zq * sq, zk * sk
        rq = lax.rsqrt(jnp.sum(aq * aq, -1, keepdims=True) + 1e-06)
        rk = lax.rsqrt(jnp.sum(ak * ak, -1, keepdims=True) + 1e-06)
        daq = rq * (SCALE * dq - q * (jnp.sum(q * dq, -1, keepdims=True) * (1.0 / SCALE)))
        dak = rk * (dk - k * jnp.sum(k * dk, -1, keepdims=True))
        dzs[0, 8 : 8 + rows, lanes] = daq * (sq * (1.0 + zq * (1.0 - sq)))
        dzs[1, 8 : 8 + rows, lanes] = dak * (sk * (1.0 + zk * (1.0 - sk)))
        dzs[2, 8 : 8 + rows, lanes] = dv * (sv * (1.0 + zv * (1.0 - sv)))
    for m in range(3):
        dz = dzs[m, 8 : 8 + rows]
        dx = None
        spill = None
        for j in range(KW):
            tap = cw_ref[m, j : j + 1]
            term = tap * dzs[m, 11 - j : 11 - j + rows]
            first = tap * dzs[m, 3 - j : 11 - j]
            dx = term if dx is None else dx + term
            spill = first if spill is None else spill + first
            tap = jnp.sum(dz * ext[m, 5 + j : 5 + j + rows], 0, keepdims=True)
            taps_ref[m, j : j + 1] = tap
        out_ref[m] = dx.astype(BF16)
        tail_ref[m] = dx[rows - 16 :]
        spill_ref[m] = spill


def output_kernel(me_ref, grad_ref, tail_ref, spill_ref, w_ref, o0, o1, o2, o3, lhs, fixed):
    rows = grad_ref.shape[1]
    part = rows // 4

    @pl.when(pl.program_id(0) == 0)
    def _():
        fixed[...] = grad_ref[...]
        for m in range(3):
            add = jnp.concatenate([jnp.zeros((8, spill_ref.shape[2]), F32), spill_ref[m]], 0)
            fixed[m, rows - 16 :] = (tail_ref[m] + add).astype(BF16)
        for k in range(4):
            at = pl.multiple_of(lax.rem(me_ref[3] + k, 4) * part, part)
            for m in range(3):
                lhs[m, k * part : (k + 1) * part] = fixed[m, pl.ds(at, part)]

    total = dot(lhs[0], w_ref[0], NT) + dot(lhs[1], w_ref[1], NT) + dot(lhs[2], w_ref[2], NT)
    o0[...] = total[:part]
    for k, ref in ((1, o1), (2, o2), (3, o3)):
        ref[...] = total[k * part : (k + 1) * part].astype(BF16)


def body(inputs, projection, conv_weight, gate_code, beta_code, grad_out):
    n = lax.axis_size("ctx")
    heads = lax.axis_size("head")
    rows, width = inputs.shape
    lanes = projection.shape[2]
    blocks = rows // BLOCK
    at = lax.axis_index("ctx")
    me = jnp.stack([at % 2, (at // 2) % XS, at // (2 * XS), lax.axis_index("head")]).astype(
        jnp.int32
    )

    def swap(block, bit):
        return lax.ppermute(block, "ctx", [(i, i ^ bit) for i in range(n)])

    def turn(block, stride, k):
        route = []
        for i in range(n):
            place = (i // stride) % 4
            route.append((i, i + ((place + k) % 4 - place) * stride))
        return lax.ppermute(block, "ctx", route)


    projected, tail = pl.pallas_call(
        project_kernel,
        in_specs=[pl.BlockSpec(memory_space=pl.ANY)] * 2,
        out_specs=(pl.BlockSpec(memory_space=pltpu.VMEM),) * 2,
        out_shape=(shape((3, rows, lanes), BF16), shape((3, 8, lanes))),
        scratch_shapes=[
            pltpu.VMEM((rows, width), BF16),
            pltpu.VMEM((3, width, lanes), BF16),
            pltpu.SemaphoreType.DMA((4,)),
        ],
        compiler_params=pltpu.CompilerParams(vmem_limit_bytes=66_500_000),
    )(inputs, projection)
    halo = lax.ppermute(tail, "ctx", [(i, i + 1) for i in range(n - 1)])
    square = (2, rows, rows)
    tall = (2, rows, DK)
    triple = (3, DK, DK)
    keep, send, z, q, k, w, u, p, d, a, t, col = call(
        local_kernel,
        (
            shape(triple), shape(triple), shape((3, rows, lanes)), shape(tall), shape(tall),
            shape(tall), shape(tall), shape(square), shape(square), shape(square),
            shape((2, blocks, BLOCK, BLOCK)), shape((2, 3, rows, DK)),
        ),
        scratch=(pltpu.VMEM((3, rows + 8, lanes), F32), pltpu.VMEM((2, 3, DK, DK), F32)),
        smem=1,
        flops=2_000_000_000,
    )(me, projected, halo, conv_weight, gate_code, beta_code, grad_out)
    recv = swap(send, 1)
    dr, e = call(adjoint_kernel, (shape(tall), shape(tall)), flops=500_000_000)(
        p, a, t, k, col, grad_out
    )
    group = call(pair_kernel, shape(triple, BF16), smem=1)(me, keep, recv)
    pre, suf, whole = call(
        group_kernel,
        (shape((2, DK, DK)), shape((2, DK, DK)), shape(triple, BF16)),
        scratch=(pltpu.VMEM((XS, 3, DK, DK), BF16),),
        smem=1,
    )(me, group, *(turn(group, 2, k) for k in (1, 2, 3)))
    near = swap(whole, 2 * XS)
    far = call(merge_kernel, (shape((2, DK, DK), BF16),) * 3, smem=1)(me, whole, near)
    far = [turn(block, 4 * XS, k) for k, block in enumerate(far, 1)]
    own, other = call(enter_kernel, (shape((2, DK, DK)), shape((2, DK, DK))), smem=1)(
        me, *far, near, pre, suf, keep, recv
    )
    other = swap(other, 1)
    rounded, edge, spill, taps = call(
        backward_kernel,
        (
            shape((3, rows, lanes), BF16), shape((3, 16, lanes)), shape((3, 8, lanes)),
            shape((3, KW, lanes)),
        ),
        scratch=(
            pltpu.VMEM((3, rows + 8, lanes), F32),
            pltpu.VMEM((3, rows + 16, lanes), F32),
        ),
        smem=1,
        flops=2_000_000_000,
    )(me, own, other, projected, halo, conv_weight, grad_out, z, q, k, w, u, d, col, dr, e)
    spill = lax.ppermute(spill, "ctx", [(i + 1, i) for i in range(n - 1)])
    part = rows // heads
    step = 512
    out = pl.BlockSpec((part, step), lambda i: (0, i))
    mine, *sends = pl.pallas_call(
        output_kernel,
        grid=(width // step,),
        in_specs=[
            pl.BlockSpec(memory_space=pltpu.SMEM),
            pl.BlockSpec((3, rows, lanes), lambda i: (0, 0, 0)),
            pl.BlockSpec((3, 16, lanes), lambda i: (0, 0, 0)),
            pl.BlockSpec((3, 8, lanes), lambda i: (0, 0, 0)),
            pl.BlockSpec((3, step, lanes), lambda i: (0, i, 0)),
        ],
        out_specs=(out,) * 4,
        out_shape=(shape((part, width)),) + (shape((part, width), BF16),) * 3,
        scratch_shapes=[pltpu.VMEM((3, rows, lanes), BF16)] * 2,
        compiler_params=pltpu.CompilerParams(vmem_limit_bytes=LIMIT),
        cost_estimate=pl.CostEstimate(
            flops=2 * 3 * rows * lanes * width, bytes_accessed=4_000_000, transcendentals=0
        ),
    )(me, rounded, edge, spill, projection)
    total = mine
    for shift, block in enumerate(sends, 1):
        got = lax.ppermute(block, "head", [(i, (i + shift) % heads) for i in range(heads)])
        total = total + got.astype(F32)
    zs = n // (2 * XS)
    column = [[z * 2 * XS + i for z in range(zs)] for i in range(2 * XS)]
    taps = taps + swap(taps, 1)
    r1, r2, r3 = (turn(taps, 2, k) for k in (1, 2, 3))
    taps = (taps + r2) + (r1 + r3)
    taps = jnp.broadcast_to(taps, (zs,) + taps.shape)
    taps = lax.all_to_all(taps, "ctx", 0, 0, axis_index_groups=column)
    taps = jnp.sum(taps, 0)
    return (total.astype(BF16), taps)


def solution(mesh):
    return jax.shard_map(
        body,
        mesh=mesh,
        in_specs=(
            P("ctx", None),
            P(None, None, "head"),
            P(None, None, "head"),
            P("head", "ctx"),
            P("head", "ctx"),
            P("ctx", "head"),
        ),
        out_specs=(P(("ctx", "head"), None), P(None, None, "head")),
        check_vma=False,
    )
```

```python
import jax
import jax.numpy as jnp
from jax import lax
from jax.experimental import pallas as pl
from jax.experimental.pallas import tpu as pltpu
from jax.sharding import PartitionSpec as P


DK = 128
KW = 4
BLOCK = 64
XS = 4
LIMIT = 20 * 2**20
SCALE = DK**-0.5
F32 = jnp.float32
BF16 = jnp.bfloat16
NN = (((1,), (0,)), ((), ()))
NT = (((1,), (1,)), ((), ()))
TN = (((0,), (0,)), ((), ()))


def split(a):
    high = a.astype(BF16)
    return high, (a - high.astype(F32)).astype(BF16)


def dot(a, b, dims):
    return lax.dot_general(a, b, dims, preferred_element_type=F32)


def mm(a, b, dims=NN):
    ah, al = split(a)
    bh, bl = split(b)
    return dot(ah, bh, dims) + (dot(ah, bl, dims) + dot(al, bh, dims))


def mm_left(a, b, dims=NN):
    ah, al = split(a)
    return dot(ah, b, dims) + dot(al, b, dims)


def mm_right(a, b, dims=NN):
    bh, bl = split(b)
    return dot(a, bh, dims) + dot(a, bl, dims)


def pieces(a):
    high, low = split(a)
    return high, low, (a - high.astype(F32) - low.astype(F32)).astype(BF16)


def iotas(rows, cols):
    return (
        lax.broadcasted_iota(jnp.int32, (rows, cols), 0),
        lax.broadcasted_iota(jnp.int32, (rows, cols), 1),
    )


def eye(n):
    r, c = iotas(n, n)
    return (r == c).astype(F32)


def call(kernel, out_shape, scratch=(), smem=0, flops=0, **kw):
    def run(*args):
        specs = [
            pl.BlockSpec(memory_space=pltpu.SMEM if i < smem else pltpu.VMEM)
            for i in range(len(args))
        ]
        return pl.pallas_call(
            kernel,
            out_shape=out_shape,
            in_specs=specs,
            out_specs=jax.tree.map(lambda _: pl.BlockSpec(memory_space=pltpu.VMEM), out_shape),
            scratch_shapes=list(scratch),
            cost_estimate=pl.CostEstimate(
                flops=flops, bytes_accessed=4_000_000, transcendentals=0
            ),
            compiler_params=pltpu.CompilerParams(vmem_limit_bytes=LIMIT),
            **kw,
        )(*args)

    return run


def shape(s, d=F32):
    return jax.ShapeDtypeStruct(s, d)


def edge_kernel(x_ref, o_ref):
    o_ref[...] = x_ref[...]


def project_kernel(x_ref, before_ref, w_ref, o_ref, halo_ref):
    for m in range(3):
        o_ref[m] = dot(x_ref[...], w_ref[m], NN).astype(BF16)
        halo = dot(before_ref[...], w_ref[m], NN).astype(BF16).astype(F32)
        halo_ref[m] = halo


def sigmoid(z):
    return 1.0 / (1.0 + jnp.exp(-z))


def local_kernel(
    me_ref, proj_ref, halo_ref, cw_ref, gate_ref, beta_ref, grad_ref,
    keep_ref, send_ref, z_ref, q_ref, k_ref, w_ref, u_ref, p_ref, d_ref, a_ref, t_ref, col_ref,
    ext, buf,
):
    rows = proj_ref.shape[1]
    blocks = rows // BLOCK
    for m in range(3):
        ext[m, 0:8] = halo_ref[m]
        ext[m, 8 : 8 + rows] = proj_ref[m].astype(F32)
    act = []
    for m in range(3):
        z = cw_ref[m, 0:1] * ext[m, 5 : 5 + rows]
        for j in range(1, KW):
            z = z + cw_ref[m, j : j + 1] * ext[m, 5 + j : 5 + j + rows]
        z_ref[m] = z
        act.append(z * sigmoid(z))
    logs = jnp.log(1.0 - 0.001 * gate_ref[...].astype(F32) / 1023.0)
    beta = beta_ref[...].astype(F32) / 1023.0
    r, c = iotas(rows, rows)
    tri = jnp.where(r >= c, 1.0, 0.0).astype(BF16)
    unit = jnp.where(r == c, 1.0, 0.0).astype(BF16)
    col = sum(dot(tri, piece, NT) for piece in pieces(logs))
    row = sum(dot(piece, tri, NT) for piece in pieces(logs))
    betas = sum(dot(unit, piece, NT) for piece in pieces(beta))
    diag = []
    keys = []
    queries = []
    for h in range(2):
        lanes = slice(h * DK, (h + 1) * DK)
        aq = act[0][:, lanes]
        ak = act[1][:, lanes]
        queries.append(aq * lax.rsqrt(jnp.sum(aq * aq, -1, keepdims=True) + 1e-06) * SCALE)
        keys.append(ak * lax.rsqrt(jnp.sum(ak * ak, -1, keepdims=True) + 1e-06))
        b = col[:, h : h + 1]
        bt = betas[:, h : h + 1]
        decay = jnp.where(r >= c, jnp.exp(b - row[h : h + 1]), 0.0)
        d_ref[h] = decay
        gram = mm(keys[h], keys[h], NT)
        low = jnp.where(r > c, decay * gram * bt, 0.0)
        a_ref[h] = low
        p_ref[h] = decay * mm(queries[h], keys[h], NT)
        q_ref[h] = queries[h]
        k_ref[h] = keys[h]
        total = col[rows - 1 : rows, h : h + 1]
        col_ref[h, 0] = jnp.broadcast_to(jnp.exp(b), (rows, DK))
        col_ref[h, 1] = jnp.broadcast_to(bt, (rows, DK))
        col_ref[h, 2] = jnp.broadcast_to(jnp.exp(total - b), (rows, DK))
        for i in range(blocks):
            span = slice(i * BLOCK, (i + 1) * BLOCK)
            diag.append(low[span, span])
    lower = jnp.stack(diag)
    count = len(diag)
    tiles = []
    for k in range(BLOCK // 8):
        rr = lax.broadcasted_iota(jnp.int32, (count, 8, BLOCK), 1) + 8 * k
        cc = lax.broadcasted_iota(jnp.int32, (count, 8, BLOCK), 2)
        tiles.append((rr == cc).astype(F32))
    for s in range(BLOCK - 1):
        k0, r0 = divmod(s, 8)
        pivot = tiles[k0][:, r0 : r0 + 1, :]
        for k in range(k0, BLOCK // 8):
            tiles[k] = tiles[k] - lower[:, 8 * k : 8 * k + 8, s : s + 1] * pivot
    inverse = jnp.concatenate(tiles, 1)
    for h in range(2):
        for i in range(blocks):
            t_ref[h, i] = inverse[h * blocks + i]
    for h in range(2):
        lanes = slice(h * DK, (h + 1) * DK)
        eb = col_ref[h, 0]
        bt = col_ref[h, 1]
        rest = col_ref[h, 2]
        rhs = jnp.concatenate([bt * eb * keys[h], bt * act[2][:, lanes]], 1)
        done = []
        for i in range(blocks):
            span = slice(i * BLOCK, (i + 1) * BLOCK)
            part = rhs[span]
            if i > 0:
                past = jnp.concatenate(done, 0) if i > 1 else done[0]
                part = part - mm(a_ref[h, span, 0 : i * BLOCK], past)
            done.append(mm(inverse[h * blocks + i], part))
        wu = jnp.concatenate(done, 0)
        w = wu[:, :DK]
        w_ref[h] = w
        u_ref[h] = wu[:, DK:]
        kt = rest * keys[h]
        ml = mm(wu, kt, TN)
        buf[h, 0] = eb[rows - 1 : rows] * eye(DK) - ml[:DK]
        buf[h, 1] = ml[DK:]
        effective = eb * queries[h] - mm(p_ref[h], w)
        buf[h, 2] = mm_right(grad_ref[:, lanes], effective, TN)
    core = me_ref[0]
    keep_ref[...] = buf[core]
    send_ref[...] = buf[1 - core]


def adjoint_kernel(p_ref, a_ref, t_ref, k_ref, col_ref, grad_ref, dr_ref, e_ref):
    rows = k_ref.shape[1]
    blocks = rows // BLOCK
    for h in range(2):
        lanes = slice(h * DK, (h + 1) * DK)
        back = mm_left(p_ref[h], grad_ref[:, lanes], TN)
        rhs = jnp.concatenate([back, col_ref[h, 2] * k_ref[h]], 1)
        done = {}
        for i in reversed(range(blocks)):
            span = slice(i * BLOCK, (i + 1) * BLOCK)
            part = rhs[span]
            for j in range(i + 1, blocks):
                below = slice(j * BLOCK, (j + 1) * BLOCK)
                wide = mm(a_ref[h, below], done[j], TN)
                part = part - wide[span]
            done[i] = mm(t_ref[h, i], part, TN)
        full = jnp.concatenate([done[i] for i in range(blocks)], 0)
        dr_ref[h] = full[:, :DK]
        e_ref[h] = full[:, DK:]


def ordered_pair(me_ref, keep_ref, recv_ref):
    first = me_ref[0] == 0
    keep, recv = keep_ref[...], recv_ref[...]
    return jnp.where(first, keep, recv), jnp.where(first, recv, keep)


def pair_kernel(me_ref, keep_ref, recv_ref, out_ref):
    e0, e1 = ordered_pair(me_ref, keep_ref, recv_ref)
    both = mm(jnp.concatenate([e0[0], e0[1]], 0), e1[0])
    out_ref[0] = (both[:DK] - eye(DK)).astype(BF16)
    out_ref[1] = (both[DK:] + e1[1]).astype(BF16)
    out_ref[2] = (mm(e1[2], e0[0], NT) + e0[2]).astype(BF16)


def group_kernel(me_ref, own_ref, r1, r2, r3, pre_ref, suf_ref, out_ref, el):
    x = me_ref[1]
    one = eye(DK)
    zero = jnp.zeros((DK, DK), F32)
    for k, ref in enumerate((own_ref, r1, r2, r3)):
        el[lax.rem(x + XS - k, XS)] = ref[...]

    def put(ref, value):
        ref[0] = value[:DK]
        ref[1] = value[DK:]

    start = jnp.concatenate([one, zero], 0)
    fwd = start
    bwd = start
    for j in range(XS):

        @pl.when(x == j)
        def _(fwd=fwd):
            put(pre_ref, fwd)

        @pl.when(x == XS - 1 - j)
        def _(bwd=bwd):
            put(suf_ref, bwd)

        mf = el[j, 0]
        mb = el[XS - 1 - j, 0]
        lf = el[j, 1].astype(F32)
        gb = el[XS - 1 - j, 2].astype(F32)
        if j == 0:
            fwd = jnp.concatenate([one + mf.astype(F32), lf], 0)
            bwd = jnp.concatenate([one + mb.astype(F32).T, gb], 0)
        else:
            fwd = fwd + mm_left(fwd, mf, NN) + jnp.concatenate([zero, lf], 0)
            bwd = bwd + mm_left(bwd, mb, NT) + jnp.concatenate([zero, gb], 0)
    out_ref[0] = (fwd[:DK] - one).astype(BF16)
    out_ref[1] = fwd[DK:].astype(BF16)
    out_ref[2] = bwd[DK:].astype(BF16)


def merge_kernel(me_ref, own_ref, recv_ref, o1, o2, o3):
    first = lax.rem(me_ref[2], 2) == 0
    pair = me_ref[2] // 2
    own, recv = own_ref[...], recv_ref[...]
    e0 = jnp.where(first, own, recv)
    e1 = jnp.where(first, recv, own)
    both = dot(jnp.concatenate([e0[0], e0[1]], 0), e1[0], NN)
    m = e0[0].astype(F32) + e1[0].astype(F32) + both[:DK]
    s = e0[1].astype(F32) + e1[1].astype(F32) + both[DK:]
    g = e0[2].astype(F32) + e1[2].astype(F32) + dot(e1[2], e0[0], NT)
    m = m.astype(BF16)
    for k, ref in ((1, o1), (2, o2), (3, o3)):
        ref[0] = m
        ref[1] = jnp.where(pair + k < 4, s, g).astype(BF16)


def enter_kernel(
    me_ref, r1, r2, r3, near_ref, pre_ref, suf_ref, keep_ref, recv_ref, own_ref, send_ref
):
    z = me_ref[2]
    pair = z // 2
    first = lax.rem(z, 2) == 0
    s = jnp.zeros((DK, DK), F32)
    g = jnp.zeros((DK, DK), F32)
    for k, ref in ((3, r3), (2, r2), (1, r1)):
        add = ref[1].astype(F32)
        new = add if k == 3 else s + mm_left(s, ref[0], NN) + add
        s = jnp.where(k <= pair, new, s)
    for k, ref in ((1, r1), (2, r2), (3, r3)):
        add = ref[1].astype(F32)
        new = add if k == 1 else g + mm_left(g, ref[0], NT) + add
        g = jnp.where(k > pair, new, g)
    near = near_ref[0]
    s = jnp.where(first, s, s + mm_left(s, near, NN) + near_ref[1].astype(F32))
    g = jnp.where(first, g + mm_left(g, near, NT) + near_ref[2].astype(F32), g)
    s = mm(s, pre_ref[0]) + pre_ref[1]
    g = mm(g, suf_ref[0]) + suf_ref[1]
    e0, e1 = ordered_pair(me_ref, keep_ref, recv_ref)
    s1 = mm(s, e0[0]) + e0[1]
    g0 = mm(g, e1[0], NT) + e1[2]
    first = me_ref[0] == 0
    own_ref[0] = jnp.where(first, s, s1)
    own_ref[1] = jnp.where(first, g0, g)
    send_ref[0] = jnp.where(first, s1, s)
    send_ref[1] = jnp.where(first, g, g0)


def backward_kernel(
    me_ref, own_ref, recv_ref, proj_ref, halo_ref, cw_ref, grad_ref,
    z_ref, q_ref, k_ref, w_ref, u_ref, d_ref, col_ref, dr_ref, e_ref,
    out_ref, tail_ref, spill_ref, taps_ref,
    ext, dzs,
):
    rows = proj_ref.shape[1]
    core = me_ref[0]
    r, c = iotas(rows, rows)
    pads = jnp.zeros((8, dzs.shape[2]), F32)
    for m in range(3):
        ext[m, 0:8] = halo_ref[m]
        ext[m, 8 : 8 + rows] = proj_ref[m].astype(F32)
        dzs[m, 0:8] = pads
        dzs[m, 8 + rows : 16 + rows] = pads
    for h in range(2):
        lanes = slice(h * DK, (h + 1) * DK)
        mine = core == h
        s = jnp.where(mine, own_ref[0], recv_ref[0])
        g = jnp.where(mine, own_ref[1], recv_ref[1])
        q, k = q_ref[h], k_ref[h]
        eb, bt, rest = col_ref[h, 0], col_ref[h, 1], col_ref[h, 2]
        do = grad_ref[:, lanes].astype(F32)
        u = u_ref[h] - mm(w_ref[h], s, NT)
        dr = dr_ref[h] + mm(e_ref[h], g, NT)
        cross = mm(jnp.concatenate([do, dr], 0), u, NT)
        decay = d_ref[h]
        x1 = decay * cross[:rows]
        da = jnp.where(r > c, decay * cross[rows:], 0.0) * -bt[:, :1]
        outer = mm(jnp.concatenate([eb * do, -(bt * eb) * dr], 0), s)
        right = mm(jnp.concatenate([x1, da], 0), k)
        dq = outer[:rows] + right[:rows]
        dk = outer[rows:] + right[rows:] + rest * mm(u, g)
        dk = dk + mm(jnp.concatenate([x1, da], 0), jnp.concatenate([q, k], 0), TN)
        dv = bt * dr
        zq = z_ref[0, :, lanes]
        zk = z_ref[1, :, lanes]
        zv = z_ref[2, :, lanes]
        sq, sk, sv = sigmoid(zq), sigmoid(zk), sigmoid(zv)
        aq, ak = zq * sq, zk * sk
        rq = lax.rsqrt(jnp.sum(aq * aq, -1, keepdims=True) + 1e-06)
        rk = lax.rsqrt(jnp.sum(ak * ak, -1, keepdims=True) + 1e-06)
        daq = rq * (SCALE * dq - q * (jnp.sum(q * dq, -1, keepdims=True) * (1.0 / SCALE)))
        dak = rk * (dk - k * jnp.sum(k * dk, -1, keepdims=True))
        dzs[0, 8 : 8 + rows, lanes] = daq * (sq * (1.0 + zq * (1.0 - sq)))
        dzs[1, 8 : 8 + rows, lanes] = dak * (sk * (1.0 + zk * (1.0 - sk)))
        dzs[2, 8 : 8 + rows, lanes] = dv * (sv * (1.0 + zv * (1.0 - sv)))
    for m in range(3):
        dz = dzs[m, 8 : 8 + rows]
        dx = None
        spill = None
        for j in range(KW):
            tap = cw_ref[m, j : j + 1]
            term = tap * dzs[m, 11 - j : 11 - j + rows]
            first = tap * dzs[m, 3 - j : 11 - j]
            dx = term if dx is None else dx + term
            spill = first if spill is None else spill + first
            tap = jnp.sum(dz * ext[m, 5 + j : 5 + j + rows], 0, keepdims=True)
            taps_ref[m, j : j + 1] = tap
        out_ref[m] = dx.astype(BF16)
        tail_ref[m] = dx[rows - 16 :]
        spill_ref[m] = spill


def output_kernel(me_ref, grad_ref, tail_ref, spill_ref, w_ref, o0, o1, o2, o3, lhs, fixed):
    rows = grad_ref.shape[1]
    part = rows // 4

    @pl.when(pl.program_id(0) == 0)
    def _():
        fixed[...] = grad_ref[...]
        for m in range(3):
            add = jnp.concatenate([jnp.zeros((8, spill_ref.shape[2]), F32), spill_ref[m]], 0)
            fixed[m, rows - 16 :] = (tail_ref[m] + add).astype(BF16)
        for k in range(4):
            at = pl.multiple_of(lax.rem(me_ref[3] + k, 4) * part, part)
            for m in range(3):
                lhs[m, k * part : (k + 1) * part] = fixed[m, pl.ds(at, part)]

    total = dot(lhs[0], w_ref[0], NT) + dot(lhs[1], w_ref[1], NT) + dot(lhs[2], w_ref[2], NT)
    o0[...] = total[:part]
    for k, ref in ((1, o1), (2, o2), (3, o3)):
        ref[...] = total[k * part : (k + 1) * part].astype(BF16)


def body(inputs, projection, conv_weight, gate_code, beta_code, grad_out):
    n = lax.axis_size("ctx")
    heads = lax.axis_size("head")
    rows, width = inputs.shape
    lanes = projection.shape[2]
    blocks = rows // BLOCK
    at = lax.axis_index("ctx")
    me = jnp.stack([at % 2, (at // 2) % XS, at // (2 * XS), lax.axis_index("head")]).astype(
        jnp.int32
    )

    def swap(block, bit):
        return lax.ppermute(block, "ctx", [(i, i ^ bit) for i in range(n)])

    def turn(block, stride, k):
        route = []
        for i in range(n):
            place = (i // stride) % 4
            route.append((i, i + ((place + k) % 4 - place) * stride))
        return lax.ppermute(block, "ctx", route)


    last = call(edge_kernel, shape((8, width), BF16), flops=200_000_000_000)(inputs[rows - 8 :])
    before = lax.ppermute(last, "ctx", [(i, i + 1) for i in range(n - 1)])
    projected, halo = call(
        project_kernel,
        (shape((3, rows, lanes), BF16), shape((3, 8, lanes))),
        flops=2_000_000_000,
    )(inputs, before, projection)
    square = (2, rows, rows)
    tall = (2, rows, DK)
    triple = (3, DK, DK)
    keep, send, z, q, k, w, u, p, d, a, t, col = call(
        local_kernel,
        (
            shape(triple), shape(triple), shape((3, rows, lanes)), shape(tall), shape(tall),
            shape(tall), shape(tall), shape(square), shape(square), shape(square),
            shape((2, blocks, BLOCK, BLOCK)), shape((2, 3, rows, DK)),
        ),
        scratch=(pltpu.VMEM((3, rows + 8, lanes), F32), pltpu.VMEM((2, 3, DK, DK), F32)),
        smem=1,
        flops=2_000_000_000,
    )(me, projected, halo, conv_weight, gate_code, beta_code, grad_out)
    recv = swap(send, 1)
    dr, e = call(adjoint_kernel, (shape(tall), shape(tall)), flops=500_000_000)(
        p, a, t, k, col, grad_out
    )
    group = call(pair_kernel, shape(triple, BF16), smem=1)(me, keep, recv)
    pre, suf, whole = call(
        group_kernel,
        (shape((2, DK, DK)), shape((2, DK, DK)), shape(triple, BF16)),
        scratch=(pltpu.VMEM((XS, 3, DK, DK), BF16),),
        smem=1,
    )(me, group, *(turn(group, 2, k) for k in (1, 2, 3)))
    near = swap(whole, 2 * XS)
    far = call(merge_kernel, (shape((2, DK, DK), BF16),) * 3, smem=1)(me, whole, near)
    far = [turn(block, 4 * XS, k) for k, block in enumerate(far, 1)]
    own, other = call(enter_kernel, (shape((2, DK, DK)), shape((2, DK, DK))), smem=1)(
        me, *far, near, pre, suf, keep, recv
    )
    other = swap(other, 1)
    rounded, edge, spill, taps = call(
        backward_kernel,
        (
            shape((3, rows, lanes), BF16), shape((3, 16, lanes)), shape((3, 8, lanes)),
            shape((3, KW, lanes)),
        ),
        scratch=(
            pltpu.VMEM((3, rows + 8, lanes), F32),
            pltpu.VMEM((3, rows + 16, lanes), F32),
        ),
        smem=1,
        flops=2_000_000_000,
    )(me, own, other, projected, halo, conv_weight, grad_out, z, q, k, w, u, d, col, dr, e)
    spill = lax.ppermute(spill, "ctx", [(i + 1, i) for i in range(n - 1)])
    part = rows // heads
    step = 512
    out = pl.BlockSpec((part, step), lambda i: (0, i))
    mine, *sends = pl.pallas_call(
        output_kernel,
        grid=(width // step,),
        in_specs=[
            pl.BlockSpec(memory_space=pltpu.SMEM),
            pl.BlockSpec((3, rows, lanes), lambda i: (0, 0, 0)),
            pl.BlockSpec((3, 16, lanes), lambda i: (0, 0, 0)),
            pl.BlockSpec((3, 8, lanes), lambda i: (0, 0, 0)),
            pl.BlockSpec((3, step, lanes), lambda i: (0, i, 0)),
        ],
        out_specs=(out,) * 4,
        out_shape=(shape((part, width)),) + (shape((part, width), BF16),) * 3,
        scratch_shapes=[pltpu.VMEM((3, rows, lanes), BF16)] * 2,
        compiler_params=pltpu.CompilerParams(vmem_limit_bytes=LIMIT),
        cost_estimate=pl.CostEstimate(
            flops=2 * 3 * rows * lanes * width, bytes_accessed=4_000_000, transcendentals=0
        ),
    )(me, rounded, edge, spill, projection)
    total = mine
    for shift, block in enumerate(sends, 1):
        got = lax.ppermute(block, "head", [(i, (i + shift) % heads) for i in range(heads)])
        total = total + got.astype(F32)

    def around(taps, stride):
        r1, r2, r3 = (turn(taps, stride, k) for k in (1, 2, 3))
        return (taps + r2) + (r1 + r3)

    taps = taps + swap(taps, 1)
    taps = around(taps, 2)
    taps = taps + swap(taps, 2 * XS)
    taps = around(taps, 4 * XS)
    return (total.astype(BF16), taps)


def solution(mesh):
    return jax.shard_map(
        body,
        mesh=mesh,
        in_specs=(
            P("ctx", None),
            P(None, None, "head"),
            P(None, None, "head"),
            P("head", "ctx"),
            P("head", "ctx"),
            P("ctx", "head"),
        ),
        out_specs=(P(("ctx", "head"), None), P(None, None, "head")),
        check_vma=False,
    )
```
